256 devices in a mesh: dp: 8 (over x, y_lo), seq: 32 (over z, y_hi, core).
Axes of the slice: x: 4, y: 4 (y_hi: 2, y_lo: 2; y = y_hi * 2 + y_lo), z: 8, core: 2. Of those that a mesh axis runs over, the one named last changes fastest.
Arguments:
- video: bfloat16 [8, 32, 16, 160, 256], P('dp', 'seq'), may hold values from -6 to 6
- cotangent: bfloat16 [8, 32, 16, 160, 256], P('dp', 'seq'), may hold values from -6 to 6
- spatial_weight: bfloat16 [3, 3, 256, 256], replicated, may hold values from -0.125 to 0.125
- temporal_weight: bfloat16 [3, 256, 256], replicated, may hold values from -0.21875 to 0.21875
Outputs:
- video_grad: bfloat16 [8, 32, 16, 160, 256], P('dp', 'seq')
- spatial_grad: float32 [2304, 256], P('seq')
- temporal_grad: float32 [768, 256], P('seq')
The draws below stay inside these ranges and needn't reach their ends.
All inputs are finite; a program needn't handle non-finite values.
Results may differ from the reference program's by a relative error of at most 0.0054.
Values may be sent and summed in bfloat16 or wider, within the bound.
A program may use at most 128 MiB of HBM per device.

```python
import jax
import jax.numpy as jnp
from jax import lax

C = 256
W = 160
H = 16
FRAMES = 32
CLIPS = 8


def raised(values, key, source, target, shards_of, factor):
    def block_of(position):
        return (jnp.arange(values.shape[position]) // (values.shape[position] // shards_of)).reshape((-1,) + (1,) * (values.ndim - 1 - position))

    first = jax.random.permutation(key, shards_of)[block_of(target)]
    other_side = (block_of(target) + shards_of // 2) % shards_of
    return jnp.where((block_of(source) == first) | (block_of(source) == other_side), factor * values, values)


def shard_levels(rng, dims, split, least, high):
    def one(position, blocks):
        heights = jax.random.uniform(jax.random.fold_in(jax.random.fold_in(rng, 6), position), (blocks,), jnp.float32, least / len(split), high / len(split))
        return jnp.repeat(jnp.exp(heights), dims[position] // blocks).reshape((-1,) + (1,) * (len(dims) - position - 1))

    level = one(*split[0])
    for cut in split[1:]:
        level = level * one(*cut)
    return level


def centred(own_key, extent, width, most, split=(), held_as=jnp.bfloat16):
    loudness = shard_levels(own_key, extent, split, -0.22, 0.18) if split else 1.0
    result = jax.random.normal(own_key, extent, jnp.float32) * width * loudness
    return jnp.minimum(jnp.maximum(result, -most), most).astype(held_as)


def noise_with(rng, dims, deviation, bound, shards, heavy, held_as=jnp.bfloat16):
    array = deviation * jax.random.normal(rng, dims, jnp.float32)
    if shards:
        array = array * shard_levels(rng, dims, shards, -0.22, 0.18)
    return jnp.clip(raised(array, jax.random.fold_in(rng, 3), *heavy), -bound, bound).astype(held_as)


def setup_inputs(seed: int = 0) -> dict:
    keys = jax.random.split(jax.random.key(seed), 5)
    video = noise_with(keys[0], (CLIPS, FRAMES, H, W, C), 1.0, 6.0, ((0, 8), (1, 32)), (1, 4, 32, 2.75))
    cotangent = centred(keys[1], (CLIPS, FRAMES, H, W, C), 1.0, 6.0, ((0, 8), (1, 32)))
    spatial_weight = centred(keys[2], (3, 3, C, C), (9 * C) ** -0.5, 0.125)
    temporal_weight = centred(keys[3], (3, C, C), (3 * C) ** -0.5, 0.21875)
    return {"video": video, "cotangent": cotangent, "spatial_weight": spatial_weight, "temporal_weight": temporal_weight}


def spatial_frame(frame, weights):
    padded = jnp.pad(frame.astype(jnp.float32), ((1, 1), (1, 1), (0, 0)))
    total = jnp.zeros(frame.shape, jnp.float32)
    for a in range(3):
        for b in range(3):
            total = total + jnp.einsum('hwc,cd->hwd', padded[a:a + H, b:b + W], weights[a, b].astype(jnp.float32))
    return total.astype(jnp.bfloat16)

def reference(video, cotangent, spatial_weight, temporal_weight):
    frames = video.reshape(CLIPS * FRAMES, H, W, C)
    hidden = lax.map(lambda f: spatial_frame(f, spatial_weight), frames).reshape(video.shape)
    hid32 = hidden.astype(jnp.float32)
    sig = jax.nn.sigmoid(hid32)
    act = (hid32 * sig).astype(jnp.bfloat16)
    grad32 = cotangent.astype(jnp.float32)
    wt32 = temporal_weight.astype(jnp.float32)
    padded = jnp.pad(grad32, ((0, 0), (0, 2), (0, 0), (0, 0), (0, 0)))
    act_grad = jnp.zeros(hid32.shape, jnp.float32)
    for k in range(3):
        act_grad = act_grad + jnp.einsum('nthwd,cd->nthwc', padded[:, k:k + FRAMES], wt32[k])
    hidden_grad = (act_grad * sig * (1.0 + hid32 * (1.0 - sig))).astype(jnp.bfloat16)
    scale = 1.0 / jnp.sqrt(jnp.float32(CLIPS * FRAMES * H * W))
    act32 = act.astype(jnp.float32)
    taps = []
    for k in range(3):
        taps.append(jnp.einsum('nthwc,nthwd->cd', act32[:, :FRAMES - k], grad32[:, k:]))
    temporal_grad = jnp.concatenate(taps, axis=0) * scale
    sw32 = spatial_weight.astype(jnp.float32)

    def frame_back(carry, pair):
        frame, dh = pair
        dh32 = dh.astype(jnp.float32)
        xpad = jnp.pad(frame.astype(jnp.float32), ((1, 1), (1, 1), (0, 0)))
        dpad = jnp.pad(dh32, ((1, 1), (1, 1), (0, 0)))
        back = jnp.zeros(frame.shape, jnp.float32)
        parts = []
        for a in range(3):
            for b in range(3):
                back = back + jnp.einsum('hwd,cd->hwc', dpad[2 - a:2 - a + H, 2 - b:2 - b + W], sw32[a, b])
                parts.append(jnp.einsum('hwc,hwd->cd', xpad[a:a + H, b:b + W], dh32))
        return (carry + jnp.concatenate(parts, axis=0), back.astype(jnp.bfloat16))
    init = jnp.zeros((9 * C, C), jnp.float32)
    summed, backs = lax.scan(frame_back, init, (frames, hidden_grad.reshape(CLIPS * FRAMES, H, W, C)))
    video_grad = backs.reshape(video.shape)
    return (video_grad, summed * scale, temporal_grad)
```

```python
import functools
import jax
import jax.numpy as jnp
from jax import lax
from jax.sharding import PartitionSpec as P
from jax.experimental import pallas as pl
from jax.experimental.pallas import tpu as pltpu

MESH = pl.DeviceIdType.MESH
H, W, C = 16, 160, 256
POS = H * W
NQ = 8
RQ = POS // NQ
F32, BF16 = jnp.float32, jnp.bfloat16


def dot(a, b):
    return lax.dot_general(a, b, (((1,), (0,)), ((), ())), preferred_element_type=F32)


def shifted(x):
    n = x.shape[0]
    col = lax.broadcasted_iota(jnp.int32, x.shape, 0) % W
    before = jnp.where(col == 0, 0.0, pltpu.roll(x, 1, 0))
    after = jnp.where(col == W - 1, 0.0, pltpu.roll(x, n - 1, 0))
    return before, after


def body(v_ref, c_ref, sw_ref, tw_ref, vg_ref, g_ref, vcat, hgcat, cots, v_t, a_t, dsil, sw_t, tw_t,
         far_send, far_recv, near_send, near_recv):
    seq = lax.axis_index("seq")
    n_seq = lax.axis_size("seq")
    core = lax.rem(seq, 2)
    sibling = seq + 1 - 2 * core
    prev = lax.rem(seq + n_seq - 2, n_seq)
    following = lax.rem(seq + 2, n_seq)

    def rows(q):
        return pl.ds(pl.multiple_of(q * RQ, RQ), RQ)

    def far(q):
        return pltpu.make_async_remote_copy(
            src_ref=c_ref.at[rows(q)], dst_ref=cots.at[rows(q), pl.ds(2 * C, C)],
            send_sem=far_send.at[q], recv_sem=far_recv.at[q],
            device_id={"seq": prev}, device_id_type=MESH)

    def near_own(q):
        return pltpu.make_async_remote_copy(
            src_ref=c_ref.at[rows(q)], dst_ref=cots.at[rows(q), pl.ds(C, C)],
            send_sem=near_send.at[q], recv_sem=near_recv.at[q],
            device_id={"seq": sibling}, device_id_type=MESH)

    def near_pass(q):
        return pltpu.make_async_remote_copy(
            src_ref=cots.at[rows(q), pl.ds(2 * C, C)], dst_ref=cots.at[rows(q), pl.ds(C, C)],
            send_sem=near_send.at[q], recv_sem=near_recv.at[q],
            device_id={"seq": sibling}, device_id_type=MESH)

    barrier = pltpu.get_barrier_semaphore()
    for other in (following, sibling):
        pl.semaphore_signal(barrier, inc=1, device_id={"seq": other}, device_id_type=MESH)
    pl.semaphore_wait(barrier, 2)
    for q in range(NQ):
        far(q).start()

    @pl.when(core == 1)
    def _():
        for q in range(NQ):
            near_own(q).start()

    for a in range(3):
        for b in range(3):
            sw_t[a, b * C:(b + 1) * C, :] = sw_ref[a, b * C:(b + 1) * C, :].T
        live = (seq + a < n_seq).astype(F32)
        tw_t[a * C:(a + 1) * C, :] = (tw_ref[a].astype(F32) * live).astype(BF16).T

    zero = jnp.zeros((W, 3 * C), BF16)
    for ref in (vcat, hgcat):
        ref[0:W, :] = zero
        ref[W + POS:2 * W + POS, :] = zero

    def load(q, _):
        x = v_ref[rows(q), :]
        before, after = shifted(x.astype(F32))
        out = pl.ds(pl.multiple_of(W + q * RQ, W), RQ)
        vcat[out, 0:C] = before.astype(BF16)
        vcat[out, C:2 * C] = x
        vcat[out, 2 * C:] = after.astype(BF16)
        cots[rows(q), 0:C] = c_ref[rows(q), :]
        return 0
    lax.fori_loop(0, NQ, load, 0)
    for m in range(POS // C):
        v_t[:, m * C:(m + 1) * C] = v_ref[m * C:(m + 1) * C, :].T

    def forward(q, _):
        acc = jnp.zeros((RQ, C), F32)
        for a in range(3):
            acc = acc + dot(vcat[pl.ds(pl.multiple_of(q * RQ + a * W, W), RQ), :], sw_ref[a])
        v = acc.astype(BF16).astype(F32)
        s = 1.0 / (1.0 + jnp.exp(-v))
        dsil[rows(q), :] = s * (1.0 + v * (1.0 - s))
        hgcat[pl.ds(pl.multiple_of(W + q * RQ, W), RQ), 0:C] = (v * s).astype(BF16)
        return 0
    lax.fori_loop(0, NQ, forward, 0)
    for m in range(POS // C):
        a_t[:, m * C:(m + 1) * C] = hgcat[W + m * C:W + (m + 1) * C, 0:C].T

    def chunk(q, _):
        far(q).wait_recv()

        @pl.when(core == 0)
        def _():
            near_pass(q).start()
        near_own(q).wait_recv()
        grad = dot(cots[rows(q), :], tw_t[...])
        hg = (grad * dsil[rows(q), :]).astype(BF16)
        before, after = shifted(hg.astype(F32))
        out = pl.ds(pl.multiple_of(W + q * RQ, W), RQ)
        hgcat[out, 0:C] = after.astype(BF16)
        hgcat[out, C:2 * C] = hg
        hgcat[out, 2 * C:] = before.astype(BF16)
        return 0

    def put(first, index, part):
        for b in range(3):
            where = pl.ds(pl.multiple_of((index * 3 + b) * C, C), C)
            value = part[:, b * C:(b + 1) * C]
            g_ref[where, :] = value if first else g_ref[where, :] + value

    def grads(start, size, first):
        def tap(a, _):
            from_row = pl.multiple_of(start + (2 - a) * W, 32)
            put(first, a, dot(v_t[:, start:start + size], hgcat[pl.ds(from_row, size), :]))
            return 0
        lax.fori_loop(0, 3, tap, 0)
        put(first, 3, dot(a_t[:, start:start + size], cots[start:start + size, :]))

    lax.fori_loop(0, 4, chunk, 0)
    grads(0, 1024, True)
    lax.fori_loop(4, 6, chunk, 0)
    grads(1024, 512, False)
    lax.fori_loop(6, 7, chunk, 0)
    grads(1536, 512, False)
    lax.fori_loop(7, 8, chunk, 0)
    grads(2048, 512, False)
    for k in (1, 2):
        live = (seq + k < n_seq).astype(F32)
        where = slice((9 + k) * C, (10 + k) * C)
        g_ref[where, :] = g_ref[where, :] * live

    def back(q, _):
        acc = jnp.zeros((RQ, C), F32)
        for a in range(3):
            acc = acc + dot(hgcat[pl.ds(pl.multiple_of(q * RQ + (2 - a) * W, W), RQ), :], sw_t[a])
        vg_ref[rows(q), :] = acc.astype(BF16)
        return 0
    lax.fori_loop(0, NQ, back, 0)

    def drain(q, _):
        far(q).wait_send()
        near_own(q).wait_send()
        return 0
    lax.fori_loop(0, NQ, drain, 0)


def compute(v, c, sw, tw):
    vm = pl.BlockSpec(memory_space=pltpu.VMEM)
    return pl.pallas_call(
        body, name="halo_conv",
        out_shape=(jax.ShapeDtypeStruct((POS, C), BF16), jax.ShapeDtypeStruct((12 * C, C), F32)),
        in_specs=[vm] * 4, out_specs=(vm, vm),
        scratch_shapes=[
            pltpu.VMEM((POS + 2 * W, 3 * C), BF16),
            pltpu.VMEM((POS + 2 * W, 3 * C), BF16),
            pltpu.VMEM((POS, 3 * C), BF16),
            pltpu.VMEM((C, POS), BF16),
            pltpu.VMEM((C, POS), BF16),
            pltpu.VMEM((POS, C), F32),
            pltpu.VMEM((3, 3 * C, C), BF16),
            pltpu.VMEM((3 * C, C), BF16),
        ] + [pltpu.SemaphoreType.DMA((NQ,))] * 4,
        compiler_params=pltpu.CompilerParams(
            collective_id=0, has_side_effects=True, vmem_limit_bytes=56 * 2**20),
    )(v, c, sw, tw)


def shards(video, cotangent, spatial_weight, temporal_weight):
    vg, g = compute(video.reshape(POS, C), cotangent.reshape(POS, C),
                    spatial_weight.reshape(3, 3 * C, C), temporal_weight)
    scale = 1.0 / jnp.sqrt(jnp.float32(8 * 32 * POS))
    g = lax.psum_scatter(jnp.concatenate([g[:9 * C].reshape(32, 72, C), g[9 * C:].reshape(32, 24, C)], axis=1).reshape(12 * C, C),
                         "seq", scatter_dimension=0, tiled=True)
    g = lax.psum(g, "dp") * scale
    return vg.reshape(video.shape), g[:72], g[72:]


def solution(mesh):
    placed = (P("dp", "seq", None, None, None), P("dp", "seq", None, None, None), P(), P())
    return jax.shard_map(
        shards, mesh=mesh, in_specs=placed,
        out_specs=(P("dp", "seq", None, None, None), P("seq", None), P("seq", None)),
        check_vma=False)
```

```python
import functools
import jax
import jax.numpy as jnp
from jax import lax
from jax.sharding import PartitionSpec as P
from jax.experimental import pallas as pl
from jax.experimental.pallas import tpu as pltpu

MESH = pl.DeviceIdType.MESH
H, W, C = 16, 160, 256
POS = H * W
NQ = 8
RQ = POS // NQ
F32, BF16 = jnp.float32, jnp.bfloat16


def dot(a, b):
    return lax.dot_general(a, b, (((1,), (0,)), ((), ())), preferred_element_type=F32)


def shifted(x):
    n = x.shape[0]
    col = lax.broadcasted_iota(jnp.int32, x.shape, 0) % W
    before = jnp.where(col == 0, 0.0, pltpu.roll(x, 1, 0))
    after = jnp.where(col == W - 1, 0.0, pltpu.roll(x, n - 1, 0))
    return before, after


def body(scale, v_ref, c_ref, sw_ref, tw_ref, vg_ref, sg_ref, tg_ref,
         vcat, hgcat, cots, v_t, a_t, dsil, sw_t, tw_t, g_ref,
         pair_out, pair_in, a1_out, a1_in, a2_out, a2_in, b1_out, b1_in, b2_out, b2_in, last_out, last_in,
         far_send, far_recv, near_send, near_recv, pair_sems, a1_sems, a2_sems, b1_sems, b2_sems, last_send, last_recv):
    seq = lax.axis_index("seq")
    n_seq = lax.axis_size("seq")
    core = lax.rem(seq, 2)
    sibling = seq + 1 - 2 * core
    prev = lax.rem(seq + n_seq - 2, n_seq)
    following = lax.rem(seq + 2, n_seq)

    def rows(q):
        return pl.ds(pl.multiple_of(q * RQ, RQ), RQ)

    def far(q):
        return pltpu.make_async_remote_copy(
            src_ref=c_ref.at[rows(q)], dst_ref=cots.at[rows(q), pl.ds(2 * C, C)],
            send_sem=far_send.at[q], recv_sem=far_recv.at[q],
            device_id={"seq": prev}, device_id_type=MESH)

    def near_own(q):
        return pltpu.make_async_remote_copy(
            src_ref=c_ref.at[rows(q)], dst_ref=cots.at[rows(q), pl.ds(C, C)],
            send_sem=near_send.at[q], recv_sem=near_recv.at[q],
            device_id={"seq": sibling}, device_id_type=MESH)

    def near_pass(q):
        return pltpu.make_async_remote_copy(
            src_ref=cots.at[rows(q), pl.ds(2 * C, C)], dst_ref=cots.at[rows(q), pl.ds(C, C)],
            send_sem=near_send.at[q], recv_sem=near_recv.at[q],
            device_id={"seq": sibling}, device_id_type=MESH)

    dp = lax.axis_index("dp")
    x, y_lo = dp // 2, lax.rem(dp, 2)
    z, y_hi = seq // 4, lax.rem(seq // 2, 2)
    y = 2 * y_hi + y_lo

    def place(dx, dy, dz):
        to_x, to_y, to_z = lax.rem(x + dx, 4), lax.rem(y + dy, 4), lax.rem(z + dz, 8)
        return (2 * to_x + lax.rem(to_y, 2), 4 * to_z + 2 * (to_y // 2) + core)

    plane = [(dx, dy) for dx in range(4) for dy in range(4) if dx or dy]
    barrier = pltpu.get_barrier_semaphore()
    for other in (following, sibling):
        pl.semaphore_signal(barrier, inc=1, device_id={"seq": other}, device_id_type=MESH)
    for dx, dy in plane:
        pl.semaphore_signal(barrier, inc=1, device_id=place(dx, dy, 0), device_id_type=MESH)
    for dz in range(1, 8):
        pl.semaphore_signal(barrier, inc=1, device_id=place(0, 0, dz), device_id_type=MESH)
    pl.semaphore_wait(barrier, 24)
    for q in range(NQ):
        far(q).start()

    @pl.when(core == 1)
    def _():
        for q in range(NQ):
            near_own(q).start()

    for a in range(3):
        for b in range(3):
            sw_t[a, b * C:(b + 1) * C, :] = sw_ref[a, b * C:(b + 1) * C, :].T
        live = (seq + a < n_seq).astype(F32)
        tw_t[a * C:(a + 1) * C, :] = (tw_ref[a].astype(F32) * live).astype(BF16).T

    zero = jnp.zeros((W, 3 * C), BF16)
    for ref in (vcat, hgcat):
        ref[0:W, :] = zero
        ref[W + POS:2 * W + POS, :] = zero

    def load(q, _):
        x = v_ref[rows(q), :]
        before, after = shifted(x.astype(F32))
        out = pl.ds(pl.multiple_of(W + q * RQ, W), RQ)
        vcat[out, 0:C] = before.astype(BF16)
        vcat[out, C:2 * C] = x
        vcat[out, 2 * C:] = after.astype(BF16)
        cots[rows(q), 0:C] = c_ref[rows(q), :]
        return 0
    lax.fori_loop(0, NQ, load, 0)
    for m in range(POS // C):
        v_t[:, m * C:(m + 1) * C] = v_ref[m * C:(m + 1) * C, :].T

    def forward(q, _):
        acc = jnp.zeros((RQ, C), F32)
        for a in range(3):
            acc = acc + dot(vcat[pl.ds(pl.multiple_of(q * RQ + a * W, W), RQ), :], sw_ref[a])
        v = acc.astype(BF16).astype(F32)
        s = 1.0 / (1.0 + jnp.exp(-v))
        dsil[rows(q), :] = s * (1.0 + v * (1.0 - s))
        hgcat[pl.ds(pl.multiple_of(W + q * RQ, W), RQ), 0:C] = (v * s).astype(BF16)
        return 0
    lax.fori_loop(0, NQ, forward, 0)
    for m in range(POS // C):
        a_t[:, m * C:(m + 1) * C] = hgcat[W + m * C:W + (m + 1) * C, 0:C].T

    def chunk(q, _):
        far(q).wait_recv()

        @pl.when(core == 0)
        def _():
            near_pass(q).start()
        near_own(q).wait_recv()
        grad = dot(cots[rows(q), :], tw_t[...])
        hg = (grad * dsil[rows(q), :]).astype(BF16)
        before, after = shifted(hg.astype(F32))
        out = pl.ds(pl.multiple_of(W + q * RQ, W), RQ)
        hgcat[out, 0:C] = after.astype(BF16)
        hgcat[out, C:2 * C] = hg
        hgcat[out, 2 * C:] = before.astype(BF16)
        return 0

    def put(first, index, part):
        for b in range(3):
            where = pl.ds(pl.multiple_of((index * 3 + b) * C, C), C)
            value = part[:, b * C:(b + 1) * C]
            g_ref[where, :] = value if first else g_ref[where, :] + value

    def grads(start, size, first):
        def tap(a, _):
            from_row = pl.multiple_of(start + (2 - a) * W, 32)
            put(first, a, dot(v_t[:, start:start + size], hgcat[pl.ds(from_row, size), :]))
            return 0
        lax.fori_loop(0, 3, tap, 0)
        put(first, 3, dot(a_t[:, start:start + size], cots[start:start + size, :]))

    lax.fori_loop(0, 4, chunk, 0)
    grads(0, 1024, True)
    lax.fori_loop(4, 6, chunk, 0)
    grads(1024, 512, False)
    lax.fori_loop(6, 7, chunk, 0)
    grads(1536, 512, False)
    lax.fori_loop(7, 8, chunk, 0)
    grads(2048, 512, False)
    def back(q, _):
        acc = jnp.zeros((RQ, C), F32)
        for a in range(3):
            acc = acc + dot(hgcat[pl.ds(pl.multiple_of(q * RQ + (2 - a) * W, W), RQ), :], sw_t[a])
        vg_ref[rows(q), :] = acc.astype(BF16)
        return 0
    def own(g, parity):
        return (pl.ds(pl.multiple_of(144 * g + 72 * parity, 8), 72),
                pl.ds(pl.multiple_of(9 * C + 48 * g + 24 * parity, 8), 24))

    def masked(g, parity):
        row = 48 * g + 24 * parity + lax.broadcasted_iota(jnp.int32, (24, C), 0)
        tap = row // C
        return jnp.where(seq + tap < n_seq, 1.0, 0.0)

    def give(g, _):
        s_rows, t_rows = own(g, 1 - core)
        pair_out[g, 0:72, :] = g_ref[s_rows, :].astype(BF16)
        pair_out[g, 72:96, :] = (g_ref[t_rows, :] * masked(g, 1 - core)).astype(BF16)
        return 0
    lax.fori_loop(0, 16, give, 0)
    pair = pltpu.make_async_remote_copy(
        src_ref=pair_out, dst_ref=pair_in, send_sem=pair_sems.at[0], recv_sem=pair_sems.at[1],
        device_id={"seq": sibling}, device_id_type=MESH)
    pair.start()
    lax.fori_loop(0, 1, back, 0)
    pair.wait_recv()

    def take(g, _):
        s_rows, t_rows = own(g, core)
        s_sum = g_ref[s_rows, :] + pair_in[g, 0:72, :].astype(F32)
        t_sum = g_ref[t_rows, :] * masked(g, core) + pair_in[g, 72:96, :].astype(F32)
        a1_out[g, :, :] = s_sum[0:64].astype(BF16)
        b1_out[g, 0:8, :] = s_sum[64:72].astype(BF16)
        b1_out[g, 8:32, :] = t_sum.astype(BF16)
        return 0
    lax.fori_loop(0, 16, take, 0)

    def quarter(at):
        return pl.ds(pl.multiple_of(16 * at, 16), 16)

    def a1(d):
        return pltpu.make_async_remote_copy(
            src_ref=a1_out.at[:, quarter(lax.rem(x + d, 4)), :], dst_ref=a1_in.at[d - 1],
            send_sem=a1_sems.at[0, d - 1], recv_sem=a1_sems.at[1, d - 1],
            device_id=place(d, 0, 0), device_id_type=MESH)

    def b1(d):
        return pltpu.make_async_remote_copy(
            src_ref=b1_out.at[pl.ds(2 * lax.rem(z + d, 8), 2)], dst_ref=b1_in.at[d - 1],
            send_sem=b1_sems.at[0, d - 1], recv_sem=b1_sems.at[1, d - 1],
            device_id=place(0, 0, d), device_id_type=MESH)

    def a2(d):
        return pltpu.make_async_remote_copy(
            src_ref=a2_out.at[pl.ds(2 * lax.rem(z + d, 8), 2)], dst_ref=a2_in.at[d - 1],
            send_sem=a2_sems.at[0, d - 1], recv_sem=a2_sems.at[1, d - 1],
            device_id=place(0, 0, d), device_id_type=MESH)

    def b2(d):
        return pltpu.make_async_remote_copy(
            src_ref=b2_out.at[lax.rem(x + d, 4)], dst_ref=b2_in.at[d - 1],
            send_sem=b2_sems.at[0, d - 1], recv_sem=b2_sems.at[1, d - 1],
            device_id=place(d, 0, 0), device_id_type=MESH)

    for d in range(1, 4):
        a1(d).start()
    for d in range(1, 8):
        b1(d).start()
    lax.fori_loop(1, 5, back, 0)
    for d in range(1, 8):
        b1(d).wait_recv()
    b_sum = b1_out[pl.ds(2 * z, 2), :, :].astype(F32)
    for d in range(1, 8):
        b_sum = b_sum + b1_in[d - 1].astype(F32)
    for q in range(4):
        b2_out[q, :, :, :] = b_sum[:, 8 * q:8 * q + 8, :]
    for d in range(1, 4):
        b2(d).start()
    for d in range(1, 4):
        a1(d).wait_recv()

    def a_add(g, _):
        total = a1_out[g, quarter(x), :].astype(F32)
        for d in range(3):
            total = total + a1_in[d, g, :, :].astype(F32)
        a2_out[g, :, :] = total.astype(BF16)
        return 0
    lax.fori_loop(0, 16, a_add, 0)
    for d in range(1, 8):
        a2(d).start()
    lax.fori_loop(5, 7, back, 0)
    for d in range(1, 4):
        b2(d).wait_recv()
    b_sum = b2_out[x, :, :, :]
    for d in range(3):
        b_sum = b_sum + b2_in[d]
    for d in range(1, 8):
        a2(d).wait_recv()
    a_sum = a2_out[pl.ds(2 * z, 2), :, :].astype(F32)
    for d in range(7):
        a_sum = a_sum + a2_in[d].astype(F32)
    last_out[:, 0:16, :] = a_sum.astype(BF16)
    last_out[:, 16:24, :] = b_sum.astype(BF16)
    me = 4 * x + y

    def last(n):
        dx, dy = plane[n]
        return pltpu.make_async_remote_copy(
            src_ref=last_out.at[lax.rem(y + dy, 4) // 2], dst_ref=last_in.at[me],
            send_sem=last_send.at[n], recv_sem=last_recv.at[me],
            device_id=place(dx, dy, 0), device_id_type=MESH)

    def last_from(n):
        dx, dy = plane[n]
        other = 4 * lax.rem(x + dx, 4) + lax.rem(y + dy, 4)
        return pltpu.make_async_remote_copy(
            src_ref=last_out.at[0], dst_ref=last_in.at[other],
            send_sem=last_send.at[n], recv_sem=last_recv.at[other],
            device_id=place(dx, dy, 0), device_id_type=MESH)

    for n in range(15):
        last(n).start()
    last_in[me, :, :] = last_out[y_hi, :, :]
    lax.fori_loop(7, NQ, back, 0)
    for n in range(15):
        last_from(n).wait_recv()
    for q in range(4):
        total = last_in[4 * q].astype(F32)
        for k in range(1, 4):
            total = total + last_in[4 * q + k].astype(F32)
        total = total * scale
        sg_ref[16 * q:16 * q + 16, :] = total[0:16]
        if q == 0:
            sg_ref[64:72, :] = total[16:24]
        else:
            tg_ref[8 * q - 8:8 * q, :] = total[16:24]
    pair.wait_send()
    for d in range(1, 4):
        a1(d).wait_send()
        b2(d).wait_send()
    for d in range(1, 8):
        b1(d).wait_send()
        a2(d).wait_send()
    for n in range(15):
        last(n).wait_send()

    def drain(q, _):
        far(q).wait_send()
        near_own(q).wait_send()
        return 0
    lax.fori_loop(0, NQ, drain, 0)


def compute(v, c, sw, tw, scale):
    vm = pl.BlockSpec(memory_space=pltpu.VMEM)
    dma = pltpu.SemaphoreType.DMA
    return pl.pallas_call(
        functools.partial(body, scale), name="halo_conv",
        out_shape=(jax.ShapeDtypeStruct((POS, C), BF16), jax.ShapeDtypeStruct((72, C), F32),
                   jax.ShapeDtypeStruct((24, C), F32)),
        in_specs=[vm] * 4, out_specs=(vm, vm, vm),
        scratch_shapes=[
            pltpu.VMEM((POS + 2 * W, 3 * C), BF16),
            pltpu.VMEM((POS + 2 * W, 3 * C), BF16),
            pltpu.VMEM((POS, 3 * C), BF16),
            pltpu.VMEM((C, POS), BF16),
            pltpu.VMEM((C, POS), BF16),
            pltpu.VMEM((POS, C), F32),
            pltpu.VMEM((3, 3 * C, C), BF16),
            pltpu.VMEM((3 * C, C), BF16),
            pltpu.VMEM((12 * C, C), F32),
            pltpu.VMEM((16, 96, C), BF16), pltpu.VMEM((16, 96, C), BF16),
            pltpu.VMEM((16, 64, C), BF16), pltpu.VMEM((3, 16, 16, C), BF16),
            pltpu.VMEM((16, 16, C), BF16), pltpu.VMEM((7, 2, 16, C), BF16),
            pltpu.VMEM((16, 32, C), BF16), pltpu.VMEM((7, 2, 32, C), BF16),
            pltpu.VMEM((4, 2, 8, C), F32), pltpu.VMEM((3, 2, 8, C), F32),
            pltpu.VMEM((2, 24, C), BF16), pltpu.VMEM((16, 24, C), BF16),
        ] + [dma((NQ,))] * 4 + [dma((2,)), dma((2, 3)), dma((2, 7)), dma((2, 7)), dma((2, 3)), dma((15,)), dma((16,))],
        compiler_params=pltpu.CompilerParams(
            collective_id=0, has_side_effects=True, vmem_limit_bytes=56 * 2**20),
    )(v, c, sw, tw)


def shards(video, cotangent, spatial_weight, temporal_weight):
    count = lax.axis_size("dp") * lax.axis_size("seq") * POS
    vg, sg, tg = compute(video.reshape(POS, C), cotangent.reshape(POS, C),
                         spatial_weight.reshape(3, 3 * C, C), temporal_weight, count ** -0.5)
    return vg.reshape(video.shape), sg, tg


def solution(mesh):
    placed = (P("dp", "seq", None, None, None), P("dp", "seq", None, None, None), P(), P())
    return jax.shard_map(
        shards, mesh=mesh, in_specs=placed,
        out_specs=(P("dp", "seq", None, None, None), P("seq", None), P("seq", None)),
        check_vma=False)
```

```python
import functools

import jax
import jax.numpy as jnp
from jax import lax
from jax.experimental import pallas as pl
from jax.experimental.pallas import tpu as pltpu
from jax.sharding import PartitionSpec as P

MESH = pl.DeviceIdType.MESH
H, W, C = 16, 160, 256
HALF = C // 2
POS = H * W
NQ = 8
RQ = POS // NQ
F32, BF16 = jnp.float32, jnp.bfloat16
PLANE = [(dx, dy) for dx in range(4) for dy in range(4) if dx or dy]
SETS = ((0, 5), (5, 10), (10, 16))


def dot(a, b):
    return lax.dot_general(a, b, (((1,), (0,)), ((), ())), preferred_element_type=F32)


def shifted(x):
    n = x.shape[0]
    col = lax.broadcasted_iota(jnp.int32, x.shape, 0) % W
    before = jnp.where(col == 0, 0.0, pltpu.roll(x, 1, 0))
    after = jnp.where(col == W - 1, 0.0, pltpu.roll(x, n - 1, 0))
    return before, after


def body(scale, stop, v_hbm, c_hbm, sw_hbm, tw_hbm, vg_ref, sg_ref, tg_ref,
         v_ref, sw_ref, tw_ref, vcat, hgcat, cots, v_t, a_t, dsil, sw_t, tw_t, g_ref,
         pair_out, pair_in, s1_out, s1_in, s2_out, s2_in, last_out, last_in,
         far_send, far_recv, near_send, near_recv, pair_send, pair_recv, s1_send, s1_recv,
         s2_send, s2_recv, last_send, last_recv, in_sems):
    dp, seq = lax.axis_index("dp"), lax.axis_index("seq")
    n_seq = lax.axis_size("seq")
    core = lax.rem(seq, 2)
    x, y_lo = dp // 2, lax.rem(dp, 2)
    z, y_hi = seq // 4, lax.rem(seq // 2, 2)
    y = 2 * y_hi + y_lo
    sibling = seq + 1 - 2 * core
    prev = lax.rem(seq + n_seq - 2, n_seq)
    following = lax.rem(seq + 2, n_seq)

    def place(dx, dy, dz):
        to_x, to_y, to_z = (x + dx) & 3, (y + dy) & 3, (z + dz) & 7
        return (2 * to_x + (to_y & 1), 4 * to_z + (to_y & 2) + core)

    def rows(q):
        return pl.ds(pl.multiple_of(q * RQ, RQ), RQ)

    def inner(q):
        return pl.ds(pl.multiple_of(W + q * RQ, W), RQ)

    def remote(src, dst, send, recv, device):
        return pltpu.make_async_remote_copy(
            src_ref=src, dst_ref=dst, send_sem=send, recv_sem=recv, device_id=device, device_id_type=MESH)

    def far(q):
        return remote(c_hbm.at[rows(q)], cots.at[rows(q), pl.ds(2 * C, C)],
                      far_send.at[q], far_recv.at[q], {"seq": prev})

    def near_own(q):
        return remote(c_hbm.at[rows(q)], cots.at[rows(q), pl.ds(C, C)],
                      near_send.at[q], near_recv.at[q], {"seq": sibling})

    def near_pass(q):
        return remote(cots.at[rows(q), pl.ds(2 * C, C)], cots.at[rows(q), pl.ds(C, C)],
                      near_send.at[q], near_recv.at[q], {"seq": sibling})

    barrier = pltpu.get_barrier_semaphore()
    for other in (following, sibling):
        pl.semaphore_signal(barrier, inc=1, device_id={"seq": other}, device_id_type=MESH)
    for dx, dy in PLANE:
        pl.semaphore_signal(barrier, inc=1, device_id=place(dx, dy, 0), device_id_type=MESH)
    for dz in range(1, 8):
        pl.semaphore_signal(barrier, inc=1, device_id=place(0, 0, dz), device_id_type=MESH)
    loads = [pltpu.make_async_copy(v_hbm, v_ref, in_sems.at[0]),
             pltpu.make_async_copy(sw_hbm, sw_ref, in_sems.at[1]),
             pltpu.make_async_copy(tw_hbm, tw_ref, in_sems.at[2]),
             pltpu.make_async_copy(c_hbm, cots.at[:, pl.ds(0, C)], in_sems.at[3])]
    for load in loads:
        load.start()
    pl.semaphore_wait(barrier, 24)
    if stop == "b":
        for load in loads:
            load.wait()
        return
    for q in range(NQ):
        far(q).start()

    @pl.when(core == 1)
    def _():
        for q in range(NQ):
            near_own(q).start()

    zero = jnp.zeros((W, 3 * C), BF16)
    for ref in (vcat, hgcat):
        ref[0:W, :] = zero
        ref[W + POS:2 * W + POS, :] = zero
    loads[0].wait()

    def spread(q, _):
        v = v_ref[rows(q), :]
        before, after = shifted(v.astype(F32))
        vcat[inner(q), 0:C] = before.astype(BF16)
        vcat[inner(q), C:2 * C] = v
        vcat[inner(q), 2 * C:] = after.astype(BF16)
        return 0
    lax.fori_loop(0, NQ, spread, 0)
    loads[1].wait()

    def forward(q, _):
        acc = jnp.zeros((RQ, C), F32)
        for a in range(3):
            acc = acc + dot(vcat[pl.ds(pl.multiple_of(q * RQ + a * W, W), RQ), :], sw_ref[a])
        v = acc.astype(BF16).astype(F32)
        s = 1.0 / (1.0 + jnp.exp(-v))
        dsil[rows(q), :] = s * (1.0 + v * (1.0 - s))
        hgcat[inner(q), 0:C] = (v * s).astype(BF16)
        return 0
    lax.fori_loop(0, NQ, forward, 0)
    for m in range(POS // C):
        a_t[:, m * C:(m + 1) * C] = hgcat[W + m * C:W + (m + 1) * C, 0:C].T
        v_t[:, m * C:(m + 1) * C] = v_ref[m * C:(m + 1) * C, :].T

    loads[2].wait()
    lives = [(seq + k < n_seq).astype(F32) for k in range(3)]
    for a in range(3):
        for b in range(3):
            sw_t[a, b * C:(b + 1) * C, :] = sw_ref[a, b * C:(b + 1) * C, :].T
        tw_t[a * C:(a + 1) * C, :] = (tw_ref[a].astype(F32) * lives[a]).astype(BF16).T
    loads[3].wait()

    if stop == "h":
        def halo_only(q, _):
            far(q).wait_recv()

            @pl.when(core == 0)
            def _():
                near_pass(q).start()
            near_own(q).wait_recv()
            return 0
        lax.fori_loop(0, NQ, halo_only, 0)
        def drain(q, _):
            far(q).wait_send()
            near_own(q).wait_send()
            return 0
        lax.fori_loop(0, NQ, drain, 0)
        return

    def chunk(q, _):
        far(q).wait_recv()

        @pl.when(core == 0)
        def _():
            near_pass(q).start()
        near_own(q).wait_recv()
        hg = (dot(cots[rows(q), :], tw_t[...]) * dsil[rows(q), :]).astype(BF16)
        before, after = shifted(hg.astype(F32))
        hgcat[inner(q), 0:C] = after.astype(BF16)
        hgcat[inner(q), C:2 * C] = hg
        hgcat[inner(q), 2 * C:] = before.astype(BF16)
        return 0

    def back(q, _):
        acc = jnp.zeros((RQ, C), F32)
        for a in range(3):
            acc = acc + dot(hgcat[pl.ds(pl.multiple_of(q * RQ + (2 - a) * W, W), RQ), :], sw_t[a])
        vg_ref[rows(q), :] = acc.astype(BF16)
        return 0

    def chunk_back(q, _):
        chunk(q, 0)
        back(q - 1, 0)
        return 0

    def put(first, index, part):
        for b in range(3):
            where = pl.ds(pl.multiple_of((index * 3 + b) * C, C), C)
            value = part[:, b * C:(b + 1) * C]
            g_ref[where, :] = value if first else g_ref[where, :] + value

    def spatial(start, size, first):
        def tap(a, _):
            from_row = pl.multiple_of(start + (2 - a) * W, 32)
            put(first, a, dot(v_t[:, start:start + size], hgcat[pl.ds(from_row, size), :]))
            return 0
        return tap

    def temporal(start, size, first):
        part = dot(a_t[:, start:start + size], cots[start:start + size, :])
        put(first, 3, jnp.concatenate([part[:, k * C:(k + 1) * C] * lives[k] for k in range(3)], axis=1))

    chunk(0, 0)
    lax.fori_loop(1, 4, chunk_back, 0)
    lax.fori_loop(0, 3, spatial(0, 1024, True), 0)
    temporal(0, 1280, True)
    lax.fori_loop(4, 6, chunk_back, 0)
    lax.fori_loop(0, 3, spatial(1024, 512, False), 0)
    temporal(1280, 512, False)
    chunk_back(6, 0)
    lax.fori_loop(0, 3, spatial(1536, 512, False), 0)
    temporal(1792, 256, False)
    chunk(7, 0)
    temporal(2048, 512, False)

    def block(g, parity):
        return 144 * g + 72 * parity, 9 * C + 48 * g + 24 * parity

    def give(g):
        s_row, t_row = block(g, 1 - core)
        pair_out[g, 0:72, :] = g_ref[pl.ds(pl.multiple_of(s_row, 8), 72), :].astype(BF16)
        pair_out[g, 72:96, :] = g_ref[pl.ds(pl.multiple_of(t_row, 8), 24), :].astype(BF16)

    def pair(n):
        g0, g1 = SETS[n]
        return remote(pair_out.at[g0:g1], pair_in.at[g0:g1], pair_send.at[n], pair_recv.at[n], {"seq": sibling})

    final_tap = spatial(2048, 512, False)
    for n in range(3):
        final_tap(n, 0)
        for g in range(*SETS[n]):
            give(g)
        pair(n).start()
    back(6, 0)

    def finish(*copies):
        for n in range(3):
            pair(n).wait_send()
        for copy in copies:
            copy.wait_send()

        def drain(q, _):
            far(q).wait_send()
            near_own(q).wait_send()
            return 0
        lax.fori_loop(0, NQ, drain, 0)

    def whole(ref, sends, recvs, n):
        return remote(ref, ref, sends.at[n], recvs.at[n], {"seq": sibling})

    def take(r):
        for h in range(8):
            s, t = [], []
            for g in (2 * h, 2 * h + 1):
                s_row, t_row = block(g, core)
                s.append(g_ref[pl.ds(pl.multiple_of(s_row + 24 * r, 8), 24), :]
                         + pair_in[g, 24 * r:24 * r + 24, :].astype(F32))
                t.append(g_ref[pl.ds(pl.multiple_of(t_row + 8 * r, 8), 8), :]
                         + pair_in[g, 72 + 8 * r:80 + 8 * r, :].astype(F32))
            for q in range(4):
                value = jnp.concatenate([i[8 * q:8 * q + 8] for i in s] if q < 3 else t, axis=0).astype(BF16)
                for part in range(2):
                    s1_out[r, part, q, 16 * h:16 * h + 16, :] = value[:, part * HALF:(part + 1) * HALF]

    def s1(r, part, d):
        to = ((y if part else x) + d) & 3
        return remote(s1_out.at[r, part, to], s1_in.at[r, part, d - 1], s1_send.at[r], s1_recv.at[r],
                      place(0, d, 0) if part else place(d, 0, 0))

    def s2(r, d):
        return remote(s2_out.at[r, pl.ds(pl.multiple_of(16 * ((z + d) & 7), 16), 16)], s2_in.at[r, d - 1],
                      s2_send.at[r], s2_recv.at[r], place(0, 0, d))

    me = 4 * x + y

    def last(r, dx, dy):
        return remote(last_out.at[r, ((y + dy) & 3) // 2], last_in.at[r, me], last_send.at[r], last_recv.at[r],
                      place(dx, dy, 0))

    s1_all = [whole(s1_in.at[r], s1_send, s1_recv, r) for r in range(3)]
    s2_all = [whole(s2_in.at[r], s2_send, s2_recv, r) for r in range(3)]
    last_all = [whole(last_in.at[r, 0:15], last_send, last_recv, r) for r in range(3)]
    for n in range(3):
        pair(n).wait_recv()
    if stop == "p":
        back(7, 0)
        finish()
        return
    for r in range(3):
        take(r)
        for d in (2, 1, 3):
            for part in range(2):
                s1(r, part, d).start()
    back(7, 0)
    for r in range(3):
        s1_all[r].wait_recv()
        for part, mine in ((0, x), (1, y)):
            total = s1_out[r, part, mine].astype(F32)
            for d in range(3):
                total = total + s1_in[r, part, d].astype(F32)
            s2_out[r, :, part * HALF:(part + 1) * HALF] = total.astype(BF16)
        for d in (4, 3, 5, 2, 6, 1, 7):
            s2(r, d).start()
    for r in range(3):
        s2_all[r].wait_recv()
        total = s2_out[r, pl.ds(pl.multiple_of(16 * z, 16), 16), :].astype(F32)
        for d in range(7):
            total = total + s2_in[r, d].astype(F32)
        for to in range(2):
            piece = total[8 * to:8 * to + 8]
            last_out[r, to, :, :] = jnp.concatenate([piece[:, :HALF], piece[:, HALF:]], axis=0).astype(BF16)
        for dx, dy in PLANE:
            last(r, dx, dy).start()
        last_in[r, me, :, :] = last_out[r, y_hi]
    for r in range(3):
        last_all[r].wait_recv()
        for q in range(4):
            left = last_in[r, 4 * q, 0:8, :].astype(F32)
            right = last_in[r, q, 8:16, :].astype(F32)
            for k in range(1, 4):
                left = left + last_in[r, 4 * q + k, 0:8, :].astype(F32)
                right = right + last_in[r, 4 * k + q, 8:16, :].astype(F32)
            out, row = (sg_ref, 24 * r + 8 * q) if q < 3 else (tg_ref, 8 * r)
            out[row:row + 8, 0:HALF] = left * scale
            out[row:row + 8, HALF:] = right * scale
    finish(*s1_all, *s2_all, *last_all)


def hand_over(*refs):
    ins, outs, sems = refs[:3], refs[3:6], refs[6]
    views = [(0, pl.ds(n * RQ, RQ)) for n in range(NQ)] + [(1, pl.ds(0, 72)), (2, pl.ds(0, 24))]
    copies = [pltpu.make_async_copy(ins[i].at[w], outs[i].at[w], sems.at[n]) for n, (i, w) in enumerate(views)]
    for copy in copies:
        copy.start()
    for copy in copies:
        copy.wait()


def compute(v, c, sw, tw, scale, stop=None, cid=0):
    anywhere = pl.BlockSpec(memory_space=pl.ANY)
    vm = pl.BlockSpec(memory_space=pltpu.VMEM)
    dma = pltpu.SemaphoreType.DMA
    shapes = (jax.ShapeDtypeStruct((POS, C), BF16), jax.ShapeDtypeStruct((72, C), F32),
              jax.ShapeDtypeStruct((24, C), F32))
    grads = pl.pallas_call(
        functools.partial(body, scale, stop), name=f"block_grads{'' if stop is None else stop}",
        out_shape=tuple(pltpu.VMEM(t.shape, t.dtype) for t in shapes),
        in_specs=[anywhere] * 4, out_specs=(vm, vm, vm),
        scratch_shapes=[
            pltpu.VMEM((POS, C), BF16),
            pltpu.VMEM((3, 3 * C, C), BF16),
            pltpu.VMEM((3, C, C), BF16),
            pltpu.VMEM((POS + 2 * W, 3 * C), BF16),
            pltpu.VMEM((POS + 2 * W, 3 * C), BF16),
            pltpu.VMEM((POS, 3 * C), BF16),
            pltpu.VMEM((C, POS), BF16),
            pltpu.VMEM((C, POS), BF16),
            pltpu.VMEM((POS, C), F32),
            pltpu.VMEM((3, 3 * C, C), BF16),
            pltpu.VMEM((3 * C, C), BF16),
            pltpu.VMEM((12 * C, C), F32),
            pltpu.VMEM((16, 96, C), BF16), pltpu.VMEM((16, 96, C), BF16),
            pltpu.VMEM((3, 2, 4, 128, HALF), BF16), pltpu.VMEM((3, 2, 3, 128, HALF), BF16),
            pltpu.VMEM((3, 128, C), BF16), pltpu.VMEM((3, 7, 16, C), BF16),
            pltpu.VMEM((3, 2, 16, HALF), BF16), pltpu.VMEM((3, 16, 16, HALF), BF16),
        ] + [dma((NQ,))] * 4 + [dma((3,))] * 8 + [dma((4,))],
        compiler_params=pltpu.CompilerParams(
            collective_id=cid, has_side_effects=True, vmem_limit_bytes=56 * 2**20),
    )(v, c, sw, tw)
    return pl.pallas_call(
        hand_over, name="hand_over", out_shape=shapes,
        in_specs=[anywhere] * 3, out_specs=(anywhere,) * 3,
        scratch_shapes=[dma((NQ + 2,))],
    )(*[pltpu.with_memory_space_constraint(g, pltpu.VMEM) for g in grads])


def shards(video, cotangent, spatial_weight, temporal_weight):
    count = lax.axis_size("dp") * lax.axis_size("seq") * POS
    vg, sg, tg = compute(video.reshape(POS, C), cotangent.reshape(POS, C),
                         spatial_weight.reshape(3, 3 * C, C), temporal_weight, count ** -0.5)
    return vg.reshape(video.shape), sg, tg


def solution(mesh):
    placed = (P("dp", "seq", None, None, None), P("dp", "seq", None, None, None), P(), P())
    return jax.shard_map(
        shards, mesh=mesh, in_specs=placed,
        out_specs=(P("dp", "seq", None, None, None), P("seq", None), P("seq", None)),
        check_vma=False)
```

```python
import functools

import jax
import jax.numpy as jnp
from jax import lax
from jax.experimental import pallas as pl
from jax.experimental.pallas import tpu as pltpu
from jax.sharding import PartitionSpec as P

MESH = pl.DeviceIdType.MESH
H, W, C = 16, 160, 256
HALF = C // 2
POS = H * W
NQ = 8
RQ = POS // NQ
F32, BF16 = jnp.float32, jnp.bfloat16
PLANE = [(dx, dy) for dx in (2, 1, 3, 0) for dy in (2, 1, 3, 0) if dx or dy]
NP = 16
SETS = ((12, 16), (6, 12), (0, 6))


def dot(a, b):
    return lax.dot_general(a, b, (((1,), (0,)), ((), ())), preferred_element_type=F32)


def shifted(x):
    n = x.shape[0]
    col = lax.broadcasted_iota(jnp.int32, x.shape, 0) % W
    before = jnp.where(col == 0, 0.0, pltpu.roll(x, 1, 0))
    after = jnp.where(col == W - 1, 0.0, pltpu.roll(x, n - 1, 0))
    return before, after


def body(scale, heights, v_hbm, c_hbm, sw_hbm, tw_hbm, vg_ref, sg_ref, tg_ref,
         v_ref, sw_ref, tw_ref, vcat, hgcat, cots, v_t, a_t, dsil, sw_t, tw_t, g_ref,
         pair_out, pair_in, pair_t_out, pair_t_in, *more):
    n_sets = len(heights)
    s1_out, s1_in, s2_out, s2_in, last_out, last_in = (more[n_sets * i:n_sets * (i + 1)] for i in range(6))
    (far_send, far_recv, near_send, near_recv, pair_send, pair_recv, s1_send, s1_recv,
     s2_send, s2_recv, last_send, last_recv, in_sems, ready) = more[6 * n_sets:]
    offsets = [sum(heights[:r]) for r in range(n_sets)]
    dp, seq = lax.axis_index("dp"), lax.axis_index("seq")
    n_seq = lax.axis_size("seq")
    core = lax.rem(seq, 2)
    x, y_lo = dp // 2, lax.rem(dp, 2)
    z, y_hi = seq // 4, lax.rem(seq // 2, 2)
    y = 2 * y_hi + y_lo
    sibling = seq + 1 - 2 * core
    prev = lax.rem(seq + n_seq - 2, n_seq)
    following = lax.rem(seq + 2, n_seq)

    def place(dx, dy, dz):
        to_x, to_y, to_z = (x + dx) & 3, (y + dy) & 3, (z + dz) & 7
        return (2 * to_x + (to_y & 1), 4 * to_z + (to_y & 2) + core)

    def rows(q):
        return pl.ds(pl.multiple_of(q * RQ, RQ), RQ)

    def inner(q):
        return pl.ds(pl.multiple_of(W + q * RQ, W), RQ)

    def lines(p, n=1):
        return pl.ds(pl.multiple_of(p * W, W), n * W)

    def remote(src, dst, send, recv, device):
        return pltpu.make_async_remote_copy(
            src_ref=src, dst_ref=dst, send_sem=send, recv_sem=recv, device_id=device, device_id_type=MESH)

    def far(p):
        return remote(c_hbm.at[lines(p)], cots.at[lines(p), pl.ds(2 * C, C)],
                      far_send.at[p], far_recv.at[p], {"seq": prev})

    def near_own(p):
        return remote(c_hbm.at[lines(p)], cots.at[lines(p), pl.ds(C, C)],
                      near_send.at[p], near_recv.at[p], {"seq": sibling})

    def near_pass(p):
        return remote(cots.at[lines(p), pl.ds(2 * C, C)], cots.at[lines(p), pl.ds(C, C)],
                      near_send.at[p], near_recv.at[p], {"seq": sibling})

    ahead = (place(1, 0, 0), place(0, 1, 0), place(0, 0, 1))
    behind = (place(3, 0, 0), place(0, 3, 0), place(0, 0, 7))

    def greet(sem, devices):
        for device in devices:
            pl.semaphore_signal(sem, inc=1, device_id=device, device_id_type=MESH)

    barrier = pltpu.get_barrier_semaphore()
    greet(barrier, ({"seq": following}, {"seq": sibling}) + ahead)
    loads = [pltpu.make_async_copy(v_hbm, v_ref, in_sems.at[0]),
             pltpu.make_async_copy(sw_hbm, sw_ref, in_sems.at[1]),
             pltpu.make_async_copy(tw_hbm, tw_ref, in_sems.at[2]),
             pltpu.make_async_copy(c_hbm, cots.at[:, pl.ds(0, C)], in_sems.at[3])]
    for load in loads:
        load.start()
    pl.semaphore_wait(barrier, 5)
    @pl.when(core == 0)
    def _():
        for p in range(NP):
            far(p).start()

    @pl.when(core == 1)
    def _():
        for p in range(NP):
            near_own(p).start()
    greet(ready.at[0], behind)

    zero = jnp.zeros((W, 3 * C), BF16)
    for ref in (vcat, hgcat):
        ref[0:W, :] = zero
        ref[W + POS:2 * W + POS, :] = zero
    loads[0].wait()

    def spread(q, _):
        v = v_ref[rows(q), :]
        before, after = shifted(v.astype(F32))
        vcat[inner(q), 0:C] = before.astype(BF16)
        vcat[inner(q), C:2 * C] = v
        vcat[inner(q), 2 * C:] = after.astype(BF16)
        return 0
    lax.fori_loop(0, NQ, spread, 0)
    @pl.when(core == 1)
    def _():
        for p in range(NP):
            far(p).start()
    loads[1].wait()
    pl.semaphore_wait(ready.at[0], 3)
    greet(ready.at[1], ahead + behind)

    def forward(q, _):
        acc = jnp.zeros((RQ, C), F32)
        for a in range(3):
            acc = acc + dot(vcat[pl.ds(pl.multiple_of(q * RQ + a * W, W), RQ), :], sw_ref[a])
        v = acc.astype(BF16).astype(F32)
        s = 1.0 / (1.0 + jnp.exp(-v))
        dsil[rows(q), :] = s * (1.0 + v * (1.0 - s))
        hgcat[inner(q), 0:C] = (v * s).astype(BF16)
        return 0
    lax.fori_loop(0, NQ, forward, 0)
    for m in range(POS // C):
        a_t[:, m * C:(m + 1) * C] = hgcat[W + m * C:W + (m + 1) * C, 0:C].T
        v_t[:, m * C:(m + 1) * C] = v_ref[m * C:(m + 1) * C, :].T

    pl.semaphore_wait(ready.at[1], 6)
    greet(ready.at[2], ahead + behind)

    loads[2].wait()
    lives = [(seq + k < n_seq).astype(F32) for k in range(3)]
    for a in range(3):
        for b in range(3):
            sw_t[a, b * C:(b + 1) * C, :] = sw_ref[a, b * C:(b + 1) * C, :].T
        tw_t[a * C:(a + 1) * C, :] = (tw_ref[a].astype(F32) * lives[a]).astype(BF16).T
    loads[3].wait()
    pl.semaphore_wait(ready.at[2], 6)
    greet(ready.at[3], ahead + behind)

    def chunk(p, n):
        for i in range(n):
            far(p + i).wait_recv()

            @pl.when(core == 0)
            def _():
                near_pass(p + i).start()
        for i in range(n):
            near_own(p + i).wait_recv()
        hg = (dot(cots[lines(p, n), :], tw_t[...]) * dsil[lines(p, n), :]).astype(BF16)
        before, after = shifted(hg.astype(F32))
        hgcat[lines(p + 1, n), 0:C] = after.astype(BF16)
        hgcat[lines(p + 1, n), C:2 * C] = hg
        hgcat[lines(p + 1, n), 2 * C:] = before.astype(BF16)

    def back(q, _):
        acc = jnp.zeros((RQ, C), F32)
        for a in range(3):
            acc = acc + dot(hgcat[pl.ds(pl.multiple_of(q * RQ + (2 - a) * W, W), RQ), :], sw_t[a])
        vg_ref[rows(q), :] = acc.astype(BF16)
        return 0

    def chunk_back(q, _):
        chunk(2 * q, 2)
        back(q - 1, 0)
        return 0

    def put(first, index, part):
        for b in range(3):
            where = pl.ds(pl.multiple_of((index * 3 + b) * C, C), C)
            value = part[:, b * C:(b + 1) * C]
            g_ref[where, :] = value if first else g_ref[where, :] + value

    def spatial(start, size, first):
        def tap(a, _):
            from_row = pl.multiple_of(start + (2 - a) * W, 32)
            put(first, a, dot(v_t[:, start:start + size], hgcat[pl.ds(from_row, size), :]))
            return 0
        return tap

    def temporal(start, size, first):
        part = dot(a_t[:, start:start + size], cots[start:start + size, :])
        put(first, 3, jnp.concatenate([part[:, k * C:(k + 1) * C] * lives[k] for k in range(3)], axis=1))

    chunk(0, 2)
    lax.fori_loop(1, 4, chunk_back, 0)
    lax.fori_loop(0, 3, spatial(0, 1024, True), 0)
    temporal(0, 1280, True)
    pl.semaphore_wait(ready.at[3], 6)
    lax.fori_loop(4, 6, chunk_back, 0)
    lax.fori_loop(0, 3, spatial(1024, 512, False), 0)
    temporal(1280, 512, False)
    chunk_back(6, 0)
    lax.fori_loop(0, 3, spatial(1536, 512, False), 0)
    temporal(1792, 256, False)
    def block(g, parity):
        return 144 * g + 72 * parity, 9 * C + 48 * g + 24 * parity

    def pair(n):
        g0, g1 = SETS[n]
        return remote(pair_out.at[g0:g1], pair_in.at[g0:g1], pair_send.at[n], pair_recv.at[n], {"seq": sibling})

    def give(n):
        for g in range(*SETS[n]):
            s_row, _ = block(g, 1 - core)
            pair_out[g, :, :] = g_ref[pl.ds(pl.multiple_of(s_row, 8), 72), :].astype(BF16)
        pair(n).start()

    pair_t = remote(pair_t_out, pair_t_in, pair_send.at[3], pair_recv.at[3], {"seq": sibling})
    chunk(14, 1)
    spatial(2048, 512, False)(2, 0)
    give(0)
    spatial(2048, 256, False)(1, 0)
    spatial(2048, 128, False)(0, 0)
    temporal(2048, 256, False)
    chunk(15, 1)
    spatial(2304, 256, False)(1, 0)
    give(1)
    temporal(2304, 256, False)
    for h in range(8):
        t_rows = [pl.ds(pl.multiple_of(block(g, 1 - core)[1], 8), 24) for g in (2 * h, 2 * h + 1)]
        pair_t_out[48 * h:48 * h + 48, :] = jnp.concatenate([g_ref[t, :] for t in t_rows], axis=0).astype(BF16)
    pair_t.start()
    spatial(2176, 256, False)(0, 0)
    give(2)

    def finish(*copies):
        for n in range(3):
            pair(n).wait_send()
        pair_t.wait_send()
        for copy in copies:
            copy.wait_send()

        def drain(p, _):
            far(p).wait_send()
            near_own(p).wait_send()
            return 0
        lax.fori_loop(0, NP, drain, 0)

    def whole(ref, sends, recvs, n):
        return remote(ref, ref, sends.at[n], recvs.at[n], {"seq": sibling})

    def take(r, n):
        high, off = heights[r], offsets[r]
        for h in range(SETS[n][0] // 2, SETS[n][1] // 2):
            s, t = [], []
            for g in (2 * h, 2 * h + 1):
                s_row, t_row = block(g, core)
                s.append(g_ref[pl.ds(pl.multiple_of(s_row + 3 * off, 8), 3 * high), :]
                         + pair_in[g, 3 * off:3 * off + 3 * high, :].astype(F32))
                t.append(g_ref[pl.ds(pl.multiple_of(t_row + off, 8), high), :]
                         + pair_t_in[24 * g + off:24 * g + off + high, :].astype(F32))
            for q in range(4):
                pieces = [i[high * q:high * q + high] for i in s] if q < 3 else t
                value = jnp.concatenate(pieces, axis=0).astype(BF16)
                for part in range(2):
                    s1_out[r][part, q, 2 * high * h:2 * high * (h + 1), :] = value[:, part * HALF:(part + 1) * HALF]

    def s1(r, part, d):
        to = ((y if part else x) + d) & 3
        return remote(s1_out[r].at[part, to], s1_in[r].at[part, d - 1], s1_send.at[r], s1_recv.at[r],
                      place(0, d, 0) if part else place(d, 0, 0))

    def of_z(r, at):
        return pl.ds(pl.multiple_of(2 * heights[r] * at, 16), 2 * heights[r])

    def s2(r, d):
        return remote(s2_out[r].at[of_z(r, (z + d) & 7)], s2_in[r].at[d - 1],
                      s2_send.at[r], s2_recv.at[r], place(0, 0, d))

    me = 4 * x + y

    def last(r, dx, dy):
        return remote(last_out[r].at[((y + dy) & 3) // 2], last_in[r].at[me], last_send.at[r], last_recv.at[r],
                      place(dx, dy, 0))

    s1_all = [whole(s1_in[r], s1_send, s1_recv, r) for r in range(n_sets)]
    s2_all = [whole(s2_in[r], s2_send, s2_recv, r) for r in range(n_sets)]
    last_all = [whole(last_in[r].at[0:15], last_send, last_recv, r) for r in range(n_sets)]
    back(6, 0)
    pair_t.wait_recv()
    for n in range(2):
        pair(n).wait_recv()
        for r in range(n_sets):
            take(r, n)
    pair(2).wait_recv()
    for r in range(n_sets):
        take(r, 2)
        for d in (2, 1, 3):
            for part in range(2):
                s1(r, part, d).start()
    back(7, 0)
    for r in range(n_sets):
        s1_all[r].wait_recv()
        for part, mine in ((0, x), (1, y)):
            total = s1_out[r][part, mine].astype(F32)
            for d in range(3):
                total = total + s1_in[r][part, d].astype(F32)
            s2_out[r][:, part * HALF:(part + 1) * HALF] = total.astype(BF16)
        for d in (4, 3, 5, 2, 6, 1, 7):
            s2(r, d).start()
    for r in range(n_sets):
        high = heights[r]
        s2_all[r].wait_recv()
        total = s2_out[r][of_z(r, z), :].astype(F32)
        for d in range(7):
            total = total + s2_in[r][d].astype(F32)
        for to in range(2):
            piece = total[high * to:high * to + high]
            last_out[r][to, :, :] = jnp.concatenate([piece[:, :HALF], piece[:, HALF:]], axis=0).astype(BF16)
        for dx, dy in PLANE:
            last(r, dx, dy).start()
        last_in[r][me, :, :] = last_out[r][y_hi]
    for r in range(n_sets):
        high, off = heights[r], offsets[r]
        last_all[r].wait_recv()
        for q in range(4):
            left = last_in[r][4 * q, 0:high, :].astype(F32)
            right = last_in[r][q, high:2 * high, :].astype(F32)
            for k in range(1, 4):
                left = left + last_in[r][4 * q + k, 0:high, :].astype(F32)
                right = right + last_in[r][4 * k + q, high:2 * high, :].astype(F32)
            out, row = (sg_ref, 3 * off + high * q) if q < 3 else (tg_ref, off)
            out[row:row + high, 0:HALF] = left * scale
            out[row:row + high, HALF:] = right * scale
    finish(*s1_all, *s2_all, *last_all)


def hand_over(*refs):
    ins, outs, sems = refs[:3], refs[3:6], refs[6]
    views = [(0, pl.ds(n * RQ, RQ)) for n in range(NQ)] + [(1, pl.ds(0, 72)), (2, pl.ds(0, 24))]
    copies = [pltpu.make_async_copy(ins[i].at[w], outs[i].at[w], sems.at[n]) for n, (i, w) in enumerate(views)]
    for copy in copies:
        copy.start()
    for copy in copies:
        copy.wait()


def compute(v, c, sw, tw, scale):
    heights = (8, 8, 8)
    anywhere = pl.BlockSpec(memory_space=pl.ANY)
    vm = pl.BlockSpec(memory_space=pltpu.VMEM)
    dma = pltpu.SemaphoreType.DMA
    shapes = (jax.ShapeDtypeStruct((POS, C), BF16), jax.ShapeDtypeStruct((72, C), F32),
              jax.ShapeDtypeStruct((24, C), F32))
    grads = pl.pallas_call(
        functools.partial(body, scale, heights), name="block_grads",
        out_shape=tuple(pltpu.VMEM(t.shape, t.dtype) for t in shapes),
        in_specs=[anywhere] * 4, out_specs=(vm, vm, vm),
        scratch_shapes=[
            pltpu.VMEM((POS, C), BF16),
            pltpu.VMEM((3, 3 * C, C), BF16),
            pltpu.VMEM((3, C, C), BF16),
            pltpu.VMEM((POS + 2 * W, 3 * C), BF16),
            pltpu.VMEM((POS + 2 * W, 3 * C), BF16),
            pltpu.VMEM((POS, 3 * C), BF16),
            pltpu.VMEM((C, POS), BF16),
            pltpu.VMEM((C, POS), BF16),
            pltpu.VMEM((POS, C), F32),
            pltpu.VMEM((3, 3 * C, C), BF16),
            pltpu.VMEM((3 * C, C), BF16),
            pltpu.VMEM((12 * C, C), F32),
            pltpu.VMEM((16, 72, C), BF16), pltpu.VMEM((16, 72, C), BF16),
            pltpu.VMEM((384, C), BF16), pltpu.VMEM((384, C), BF16),
            *[pltpu.VMEM((2, 4, 16 * h, HALF), BF16) for h in heights],
            *[pltpu.VMEM((2, 3, 16 * h, HALF), BF16) for h in heights],
            *[pltpu.VMEM((16 * h, C), BF16) for h in heights],
            *[pltpu.VMEM((7, 2 * h, C), BF16) for h in heights],
            *[pltpu.VMEM((2, 2 * h, HALF), BF16) for h in heights],
            *[pltpu.VMEM((16, 2 * h, HALF), BF16) for h in heights],
        ] + [dma((NP,))] * 4 + [dma((4,))] * 2 + [dma((3,))] * 6 + [dma((4,)), pltpu.SemaphoreType.REGULAR((4,))],
        compiler_params=pltpu.CompilerParams(
            collective_id=0, has_side_effects=True, vmem_limit_bytes=56 * 2**20),
    )(v, c, sw, tw)
    return pl.pallas_call(
        hand_over, name="hand_over", out_shape=shapes,
        in_specs=[anywhere] * 3, out_specs=(anywhere,) * 3,
        scratch_shapes=[dma((NQ + 2,))],
    )(*[pltpu.with_memory_space_constraint(g, pltpu.VMEM) for g in grads])


def shards(video, cotangent, spatial_weight, temporal_weight):
    count = lax.axis_size("dp") * lax.axis_size("seq") * POS
    vg, sg, tg = compute(video.reshape(POS, C), cotangent.reshape(POS, C),
                         spatial_weight.reshape(3, 3 * C, C), temporal_weight, count ** -0.5)
    return vg.reshape(video.shape), sg, tg


def solution(mesh):
    placed = (P("dp", "seq", None, None, None), P("dp", "seq", None, None, None), P(), P())
    return jax.shard_map(
        shards, mesh=mesh, in_specs=placed,
        out_specs=(P("dp", "seq", None, None, None), P("seq", None), P("seq", None)),
        check_vma=False)
```

```python
import functools

import jax
import jax.numpy as jnp
from jax import lax
from jax.experimental import pallas as pl
from jax.experimental.pallas import tpu as pltpu
from jax.sharding import PartitionSpec as P

MESH = pl.DeviceIdType.MESH
H, W, C = 16, 160, 256
HALF = C // 2
POS = H * W
NQ = 8
RQ = POS // NQ
F32, BF16 = jnp.float32, jnp.bfloat16
PLANE = [(dx, dy) for dx in range(4) for dy in range(4) if dx or dy]
NP = 16
SETS = ((12, 16), (6, 12), (0, 6))


def dot(a, b):
    return lax.dot_general(a, b, (((1,), (0,)), ((), ())), preferred_element_type=F32)


def shifted(x):
    n = x.shape[0]
    col = lax.broadcasted_iota(jnp.int32, x.shape, 0) % W
    before = jnp.where(col == 0, 0.0, pltpu.roll(x, 1, 0))
    after = jnp.where(col == W - 1, 0.0, pltpu.roll(x, n - 1, 0))
    return before, after


def body(scale, heights, v_hbm, c_hbm, sw_hbm, tw_hbm, vg_ref, sg_ref, tg_ref,
         v_ref, sw_ref, tw_ref, vcat, hgcat, cots, v_t, a_t, dsil, sw_t, tw_t, g_ref,
         pair_out, pair_in, pair_t_out, pair_t_in, *more):
    n_sets = len(heights)
    s1_out, s1_in, s2_out, s2_in, last_out, last_in = (more[n_sets * i:n_sets * (i + 1)] for i in range(6))
    (far_send, far_recv, near_send, near_recv, pair_send, pair_recv, s1_send, s1_recv,
     s2_send, s2_recv, last_send, last_recv, in_sems, ready) = more[6 * n_sets:]
    offsets = [sum(heights[:r]) for r in range(n_sets)]
    dp, seq = lax.axis_index("dp"), lax.axis_index("seq")
    n_seq = lax.axis_size("seq")
    core = lax.rem(seq, 2)
    x, y_lo = dp // 2, lax.rem(dp, 2)
    z, y_hi = seq // 4, lax.rem(seq // 2, 2)
    y = 2 * y_hi + y_lo
    sibling = seq + 1 - 2 * core
    prev = lax.rem(seq + n_seq - 2, n_seq)
    following = lax.rem(seq + 2, n_seq)

    def place(dx, dy, dz):
        to_x, to_y, to_z = (x + dx) & 3, (y + dy) & 3, (z + dz) & 7
        return (2 * to_x + (to_y & 1), 4 * to_z + (to_y & 2) + core)

    def rows(q):
        return pl.ds(pl.multiple_of(q * RQ, RQ), RQ)

    def inner(q):
        return pl.ds(pl.multiple_of(W + q * RQ, W), RQ)

    def lines(p, n=1):
        return pl.ds(pl.multiple_of(p * W, W), n * W)

    def remote(src, dst, send, recv, device):
        return pltpu.make_async_remote_copy(
            src_ref=src, dst_ref=dst, send_sem=send, recv_sem=recv, device_id=device, device_id_type=MESH)

    def far(p):
        return remote(c_hbm.at[lines(p)], cots.at[lines(p), pl.ds(2 * C, C)],
                      far_send.at[p], far_recv.at[p], {"seq": prev})

    def near_own(p):
        return remote(c_hbm.at[lines(p)], cots.at[lines(p), pl.ds(C, C)],
                      near_send.at[p], near_recv.at[p], {"seq": sibling})

    def near_pass(p):
        return remote(cots.at[lines(p), pl.ds(2 * C, C)], cots.at[lines(p), pl.ds(C, C)],
                      near_send.at[p], near_recv.at[p], {"seq": sibling})

    ahead = (place(1, 0, 0), place(0, 1, 0), place(0, 0, 1))
    behind = (place(3, 0, 0), place(0, 3, 0), place(0, 0, 7))

    def greet(sem, devices):
        for device in devices:
            pl.semaphore_signal(sem, inc=1, device_id=device, device_id_type=MESH)

    barrier = pltpu.get_barrier_semaphore()
    greet(barrier, ({"seq": following}, {"seq": sibling}) + ahead)
    loads = [pltpu.make_async_copy(v_hbm, v_ref, in_sems.at[0]),
             pltpu.make_async_copy(sw_hbm, sw_ref, in_sems.at[1]),
             pltpu.make_async_copy(tw_hbm, tw_ref, in_sems.at[2]),
             pltpu.make_async_copy(c_hbm, cots.at[:, pl.ds(0, C)], in_sems.at[3])]
    for load in loads:
        load.start()
    pl.semaphore_wait(barrier, 5)
    for p in range(NP):
        far(p).start()

    @pl.when(core == 1)
    def _():
        for p in range(NP):
            near_own(p).start()
    greet(ready.at[0], behind)

    zero = jnp.zeros((W, 3 * C), BF16)
    for ref in (vcat, hgcat):
        ref[0:W, :] = zero
        ref[W + POS:2 * W + POS, :] = zero
    loads[0].wait()

    def spread(q, _):
        v = v_ref[rows(q), :]
        before, after = shifted(v.astype(F32))
        vcat[inner(q), 0:C] = before.astype(BF16)
        vcat[inner(q), C:2 * C] = v
        vcat[inner(q), 2 * C:] = after.astype(BF16)
        return 0
    lax.fori_loop(0, NQ, spread, 0)
    loads[1].wait()
    pl.semaphore_wait(ready.at[0], 3)
    greet(ready.at[1], ahead + behind)

    def forward(q, _):
        acc = jnp.zeros((RQ, C), F32)
        for a in range(3):
            acc = acc + dot(vcat[pl.ds(pl.multiple_of(q * RQ + a * W, W), RQ), :], sw_ref[a])
        v = acc.astype(BF16).astype(F32)
        s = 1.0 / (1.0 + jnp.exp(-v))
        dsil[rows(q), :] = s * (1.0 + v * (1.0 - s))
        hgcat[inner(q), 0:C] = (v * s).astype(BF16)
        return 0
    lax.fori_loop(0, NQ, forward, 0)
    for m in range(POS // C):
        a_t[:, m * C:(m + 1) * C] = hgcat[W + m * C:W + (m + 1) * C, 0:C].T
        v_t[:, m * C:(m + 1) * C] = v_ref[m * C:(m + 1) * C, :].T

    pl.semaphore_wait(ready.at[1], 6)
    greet(ready.at[2], ahead + behind)

    loads[2].wait()
    lives = [(seq + k < n_seq).astype(F32) for k in range(3)]
    for a in range(3):
        for b in range(3):
            sw_t[a, b * C:(b + 1) * C, :] = sw_ref[a, b * C:(b + 1) * C, :].T
        tw_t[a * C:(a + 1) * C, :] = (tw_ref[a].astype(F32) * lives[a]).astype(BF16).T
    loads[3].wait()
    pl.semaphore_wait(ready.at[2], 6)
    greet(ready.at[3], ahead + behind)

    def chunk(p, n):
        for i in range(n):
            far(p + i).wait_recv()

            @pl.when(core == 0)
            def _():
                near_pass(p + i).start()
        for i in range(n):
            near_own(p + i).wait_recv()
        hg = (dot(cots[lines(p, n), :], tw_t[...]) * dsil[lines(p, n), :]).astype(BF16)
        before, after = shifted(hg.astype(F32))
        hgcat[lines(p + 1, n), 0:C] = after.astype(BF16)
        hgcat[lines(p + 1, n), C:2 * C] = hg
        hgcat[lines(p + 1, n), 2 * C:] = before.astype(BF16)

    def back(q, _):
        acc = jnp.zeros((RQ, C), F32)
        for a in range(3):
            acc = acc + dot(hgcat[pl.ds(pl.multiple_of(q * RQ + (2 - a) * W, W), RQ), :], sw_t[a])
        vg_ref[rows(q), :] = acc.astype(BF16)
        return 0

    def chunk_back(q, _):
        chunk(2 * q, 2)
        back(q - 1, 0)
        return 0

    def put(first, index, part):
        for b in range(3):
            where = pl.ds(pl.multiple_of((index * 3 + b) * C, C), C)
            value = part[:, b * C:(b + 1) * C]
            g_ref[where, :] = value if first else g_ref[where, :] + value

    def spatial(start, size, first):
        def tap(a, _):
            from_row = pl.multiple_of(start + (2 - a) * W, 32)
            put(first, a, dot(v_t[:, start:start + size], hgcat[pl.ds(from_row, size), :]))
            return 0
        return tap

    def temporal(start, size, first):
        part = dot(a_t[:, start:start + size], cots[start:start + size, :])
        put(first, 3, jnp.concatenate([part[:, k * C:(k + 1) * C] * lives[k] for k in range(3)], axis=1))

    chunk(0, 2)
    lax.fori_loop(1, 4, chunk_back, 0)
    lax.fori_loop(0, 3, spatial(0, 1024, True), 0)
    temporal(0, 1280, True)
    pl.semaphore_wait(ready.at[3], 6)
    lax.fori_loop(4, 6, chunk_back, 0)
    lax.fori_loop(0, 3, spatial(1024, 512, False), 0)
    temporal(1280, 512, False)
    chunk_back(6, 0)
    lax.fori_loop(0, 3, spatial(1536, 512, False), 0)
    temporal(1792, 256, False)
    def block(g, parity):
        return 144 * g + 72 * parity, 9 * C + 48 * g + 24 * parity

    def pair(n):
        g0, g1 = SETS[n]
        return remote(pair_out.at[g0:g1], pair_in.at[g0:g1], pair_send.at[n], pair_recv.at[n], {"seq": sibling})

    def give(n):
        for g in range(*SETS[n]):
            s_row, _ = block(g, 1 - core)
            pair_out[g, :, :] = g_ref[pl.ds(pl.multiple_of(s_row, 8), 72), :].astype(BF16)
        pair(n).start()

    pair_t = remote(pair_t_out, pair_t_in, pair_send.at[3], pair_recv.at[3], {"seq": sibling})
    chunk(14, 1)
    spatial(2048, 512, False)(2, 0)
    give(0)
    spatial(2048, 256, False)(1, 0)
    spatial(2048, 128, False)(0, 0)
    temporal(2048, 256, False)
    chunk(15, 1)
    spatial(2304, 256, False)(1, 0)
    give(1)
    temporal(2304, 256, False)
    for h in range(8):
        t_rows = [pl.ds(pl.multiple_of(block(g, 1 - core)[1], 8), 24) for g in (2 * h, 2 * h + 1)]
        pair_t_out[48 * h:48 * h + 48, :] = jnp.concatenate([g_ref[t, :] for t in t_rows], axis=0).astype(BF16)
    pair_t.start()
    spatial(2176, 256, False)(0, 0)
    give(2)

    def finish(*copies):
        for n in range(3):
            pair(n).wait_send()
        pair_t.wait_send()
        for copy in copies:
            copy.wait_send()

        def drain(p, _):
            far(p).wait_send()
            near_own(p).wait_send()
            return 0
        lax.fori_loop(0, NP, drain, 0)

    def whole(ref, sends, recvs, n):
        return remote(ref, ref, sends.at[n], recvs.at[n], {"seq": sibling})

    def take(r, n):
        high, off = heights[r], offsets[r]
        for h in range(SETS[n][0] // 2, SETS[n][1] // 2):
            s, t = [], []
            for g in (2 * h, 2 * h + 1):
                s_row, t_row = block(g, core)
                s.append(g_ref[pl.ds(pl.multiple_of(s_row + 3 * off, 8), 3 * high), :]
                         + pair_in[g, 3 * off:3 * off + 3 * high, :].astype(F32))
                t.append(g_ref[pl.ds(pl.multiple_of(t_row + off, 8), high), :]
                         + pair_t_in[24 * g + off:24 * g + off + high, :].astype(F32))
            for q in range(4):
                pieces = [i[high * q:high * q + high] for i in s] if q < 3 else t
                value = jnp.concatenate(pieces, axis=0).astype(BF16)
                for part in range(2):
                    s1_out[r][part, q, 2 * high * h:2 * high * (h + 1), :] = value[:, part * HALF:(part + 1) * HALF]

    def s1(r, part, d):
        to = ((y if part else x) + d) & 3
        return remote(s1_out[r].at[part, to], s1_in[r].at[part, d - 1], s1_send.at[r], s1_recv.at[r],
                      place(0, d, 0) if part else place(d, 0, 0))

    def of_z(r, at):
        return pl.ds(pl.multiple_of(2 * heights[r] * at, 16), 2 * heights[r])

    def s2(r, d):
        return remote(s2_out[r].at[of_z(r, (z + d) & 7)], s2_in[r].at[d - 1],
                      s2_send.at[r], s2_recv.at[r], place(0, 0, d))

    me = 4 * x + y

    def last(r, dx, dy):
        return remote(last_out[r].at[((y + dy) & 3) // 2], last_in[r].at[me], last_send.at[r], last_recv.at[r],
                      place(dx, dy, 0))

    s1_all = [whole(s1_in[r], s1_send, s1_recv, r) for r in range(n_sets)]
    s2_all = [whole(s2_in[r], s2_send, s2_recv, r) for r in range(n_sets)]
    last_all = [whole(last_in[r].at[0:15], last_send, last_recv, r) for r in range(n_sets)]
    back(6, 0)
    pair_t.wait_recv()
    for n in range(2):
        pair(n).wait_recv()
        for r in range(n_sets):
            take(r, n)
    pair(2).wait_recv()
    for r in range(n_sets):
        take(r, 2)
        for d in (2, 1, 3):
            for part in range(2):
                s1(r, part, d).start()
    back(7, 0)
    for r in range(n_sets):
        s1_all[r].wait_recv()
        for part, mine in ((0, x), (1, y)):
            total = s1_out[r][part, mine].astype(F32)
            for d in range(3):
                total = total + s1_in[r][part, d].astype(F32)
            s2_out[r][:, part * HALF:(part + 1) * HALF] = total.astype(BF16)
        for d in (4, 3, 5, 2, 6, 1, 7):
            s2(r, d).start()
    for r in range(n_sets):
        high = heights[r]
        s2_all[r].wait_recv()
        total = s2_out[r][of_z(r, z), :].astype(F32)
        for d in range(7):
            total = total + s2_in[r][d].astype(F32)
        for to in range(2):
            piece = total[high * to:high * to + high]
            last_out[r][to, :, :] = jnp.concatenate([piece[:, :HALF], piece[:, HALF:]], axis=0).astype(BF16)
        for dx, dy in PLANE:
            last(r, dx, dy).start()
        last_in[r][me, :, :] = last_out[r][y_hi]
    for r in range(n_sets):
        high, off = heights[r], offsets[r]
        last_all[r].wait_recv()
        for q in range(4):
            left = last_in[r][4 * q, 0:high, :].astype(F32)
            right = last_in[r][q, high:2 * high, :].astype(F32)
            for k in range(1, 4):
                left = left + last_in[r][4 * q + k, 0:high, :].astype(F32)
                right = right + last_in[r][4 * k + q, high:2 * high, :].astype(F32)
            out, row = (sg_ref, 3 * off + high * q) if q < 3 else (tg_ref, off)
            out[row:row + high, 0:HALF] = left * scale
            out[row:row + high, HALF:] = right * scale
    finish(*s1_all, *s2_all, *last_all)


def hand_over(*refs):
    ins, outs, sems = refs[:3], refs[3:6], refs[6]
    views = [(0, pl.ds(n * RQ, RQ)) for n in range(NQ)] + [(1, pl.ds(0, 72)), (2, pl.ds(0, 24))]
    copies = [pltpu.make_async_copy(ins[i].at[w], outs[i].at[w], sems.at[n]) for n, (i, w) in enumerate(views)]
    for copy in copies:
        copy.start()
    for copy in copies:
        copy.wait()


def compute(v, c, sw, tw, scale):
    heights = (8, 8, 8)
    anywhere = pl.BlockSpec(memory_space=pl.ANY)
    vm = pl.BlockSpec(memory_space=pltpu.VMEM)
    dma = pltpu.SemaphoreType.DMA
    shapes = (jax.ShapeDtypeStruct((POS, C), BF16), jax.ShapeDtypeStruct((72, C), F32),
              jax.ShapeDtypeStruct((24, C), F32))
    grads = pl.pallas_call(
        functools.partial(body, scale, heights), name="block_grads",
        out_shape=tuple(pltpu.VMEM(t.shape, t.dtype) for t in shapes),
        in_specs=[anywhere] * 4, out_specs=(vm, vm, vm),
        scratch_shapes=[
            pltpu.VMEM((POS, C), BF16),
            pltpu.VMEM((3, 3 * C, C), BF16),
            pltpu.VMEM((3, C, C), BF16),
            pltpu.VMEM((POS + 2 * W, 3 * C), BF16),
            pltpu.VMEM((POS + 2 * W, 3 * C), BF16),
            pltpu.VMEM((POS, 3 * C), BF16),
            pltpu.VMEM((C, POS), BF16),
            pltpu.VMEM((C, POS), BF16),
            pltpu.VMEM((POS, C), F32),
            pltpu.VMEM((3, 3 * C, C), BF16),
            pltpu.VMEM((3 * C, C), BF16),
            pltpu.VMEM((12 * C, C), F32),
            pltpu.VMEM((16, 72, C), BF16), pltpu.VMEM((16, 72, C), BF16),
            pltpu.VMEM((384, C), BF16), pltpu.VMEM((384, C), BF16),
            *[pltpu.VMEM((2, 4, 16 * h, HALF), BF16) for h in heights],
            *[pltpu.VMEM((2, 3, 16 * h, HALF), BF16) for h in heights],
            *[pltpu.VMEM((16 * h, C), BF16) for h in heights],
            *[pltpu.VMEM((7, 2 * h, C), BF16) for h in heights],
            *[pltpu.VMEM((2, 2 * h, HALF), BF16) for h in heights],
            *[pltpu.VMEM((16, 2 * h, HALF), BF16) for h in heights],
        ] + [dma((NP,))] * 4 + [dma((4,))] * 2 + [dma((3,))] * 6 + [dma((4,)), pltpu.SemaphoreType.REGULAR((4,))],
        compiler_params=pltpu.CompilerParams(
            collective_id=0, has_side_effects=True, vmem_limit_bytes=56 * 2**20),
    )(v, c, sw, tw)
    return pl.pallas_call(
        hand_over, name="hand_over", out_shape=shapes,
        in_specs=[anywhere] * 3, out_specs=(anywhere,) * 3,
        scratch_shapes=[dma((NQ + 2,))],
    )(*[pltpu.with_memory_space_constraint(g, pltpu.VMEM) for g in grads])


def shards(video, cotangent, spatial_weight, temporal_weight):
    count = lax.axis_size("dp") * lax.axis_size("seq") * POS
    vg, sg, tg = compute(video.reshape(POS, C), cotangent.reshape(POS, C),
                         spatial_weight.reshape(3, 3 * C, C), temporal_weight, count ** -0.5)
    return vg.reshape(video.shape), sg, tg


def solution(mesh):
    placed = (P("dp", "seq", None, None, None), P("dp", "seq", None, None, None), P(), P())
    return jax.shard_map(
        shards, mesh=mesh, in_specs=placed,
        out_specs=(P("dp", "seq", None, None, None), P("seq", None), P("seq", None)),
        check_vma=False)
```

```python
import functools

import jax
import jax.numpy as jnp
from jax import lax
from jax.experimental import pallas as pl
from jax.experimental.pallas import tpu as pltpu
from jax.sharding import PartitionSpec as P

MESH = pl.DeviceIdType.MESH
H, W, C = 16, 160, 256
HALF = C // 2
POS = H * W
NQ = 8
RQ = POS // NQ
F32, BF16 = jnp.float32, jnp.bfloat16
PLANE = [(dx, dy) for dx in (2, 1, 3, 0) for dy in (2, 1, 3, 0) if dx or dy]
NP = 16
SETS = ((12, 16), (6, 12), (0, 6))


def dot(a, b):
    return lax.dot_general(a, b, (((1,), (0,)), ((), ())), preferred_element_type=F32)


def shifted(x):
    n = x.shape[0]
    col = lax.broadcasted_iota(jnp.int32, x.shape, 0) % W
    before = jnp.where(col == 0, 0.0, pltpu.roll(x, 1, 0))
    after = jnp.where(col == W - 1, 0.0, pltpu.roll(x, n - 1, 0))
    return before, after


def body(scale, heights, v_hbm, c_hbm, sw_hbm, tw_hbm, vg_ref, sg_ref, tg_ref,
         v_ref, sw_ref, tw_ref, vcat, hgcat, cots, v_t, a_t, dsil, sw_t, tw_t, g_ref,
         pair_out, pair_in, pair_t_out, pair_t_in, *more):
    n_sets = len(heights)
    s1_out, s1_in, s2_out, s2_in, last_out, last_in = (more[n_sets * i:n_sets * (i + 1)] for i in range(6))
    (far_send, far_recv, near_send, near_recv, pair_send, pair_recv, s1_send, s1_recv,
     s2_send, s2_recv, last_send, last_recv, in_sems, ready) = more[6 * n_sets:]
    offsets = [sum(heights[:r]) for r in range(n_sets)]
    dp, seq = lax.axis_index("dp"), lax.axis_index("seq")
    n_seq = lax.axis_size("seq")
    core = lax.rem(seq, 2)
    x, y_lo = dp // 2, lax.rem(dp, 2)
    z, y_hi = seq // 4, lax.rem(seq // 2, 2)
    y = 2 * y_hi + y_lo
    sibling = seq + 1 - 2 * core
    prev = lax.rem(seq + n_seq - 2, n_seq)
    following = lax.rem(seq + 2, n_seq)

    def place(dx, dy, dz):
        to_x, to_y, to_z = (x + dx) & 3, (y + dy) & 3, (z + dz) & 7
        return (2 * to_x + (to_y & 1), 4 * to_z + (to_y & 2) + core)

    def rows(q):
        return pl.ds(pl.multiple_of(q * RQ, RQ), RQ)

    def inner(q):
        return pl.ds(pl.multiple_of(W + q * RQ, W), RQ)

    def lines(p, n=1):
        return pl.ds(pl.multiple_of(p * W, W), n * W)

    def remote(src, dst, send, recv, device):
        return pltpu.make_async_remote_copy(
            src_ref=src, dst_ref=dst, send_sem=send, recv_sem=recv, device_id=device, device_id_type=MESH)

    def far(p):
        return remote(c_hbm.at[lines(p)], cots.at[lines(p), pl.ds(2 * C, C)],
                      far_send.at[p], far_recv.at[p], {"seq": prev})

    def near_own(p):
        return remote(c_hbm.at[lines(p)], cots.at[lines(p), pl.ds(C, C)],
                      near_send.at[p], near_recv.at[p], {"seq": sibling})

    def near_pass(p):
        return remote(cots.at[lines(p), pl.ds(2 * C, C)], cots.at[lines(p), pl.ds(C, C)],
                      near_send.at[p], near_recv.at[p], {"seq": sibling})

    ahead = (place(1, 0, 0), place(0, 1, 0), place(0, 0, 1))
    behind = (place(3, 0, 0), place(0, 3, 0), place(0, 0, 7))

    def greet(sem, devices):
        for device in devices:
            pl.semaphore_signal(sem, inc=1, device_id=device, device_id_type=MESH)

    barrier = pltpu.get_barrier_semaphore()
    greet(barrier, ({"seq": following}, {"seq": sibling}) + ahead)
    loads = [pltpu.make_async_copy(v_hbm, v_ref, in_sems.at[0]),
             pltpu.make_async_copy(sw_hbm, sw_ref, in_sems.at[1]),
             pltpu.make_async_copy(tw_hbm, tw_ref, in_sems.at[2]),
             pltpu.make_async_copy(c_hbm, cots.at[:, pl.ds(0, C)], in_sems.at[3])]
    for load in loads:
        load.start()
    pl.semaphore_wait(barrier, 5)
    @pl.when(core == 0)
    def _():
        for p in range(NP):
            far(p).start()

    @pl.when(core == 1)
    def _():
        for p in range(NP):
            near_own(p).start()
    greet(ready.at[0], behind)

    zero = jnp.zeros((W, 3 * C), BF16)
    for ref in (vcat, hgcat):
        ref[0:W, :] = zero
        ref[W + POS:2 * W + POS, :] = zero
    loads[0].wait()

    def spread(q, _):
        v = v_ref[rows(q), :]
        before, after = shifted(v.astype(F32))
        vcat[inner(q), 0:C] = before.astype(BF16)
        vcat[inner(q), C:2 * C] = v
        vcat[inner(q), 2 * C:] = after.astype(BF16)
        return 0
    lax.fori_loop(0, NQ, spread, 0)
    @pl.when(core == 1)
    def _():
        for p in range(NP):
            far(p).start()
    loads[1].wait()
    pl.semaphore_wait(ready.at[0], 3)
    greet(ready.at[1], ahead + behind)

    def forward(q, _):
        acc = jnp.zeros((RQ, C), F32)
        for a in range(3):
            acc = acc + dot(vcat[pl.ds(pl.multiple_of(q * RQ + a * W, W), RQ), :], sw_ref[a])
        v = acc.astype(BF16).astype(F32)
        s = 1.0 / (1.0 + jnp.exp(-v))
        dsil[rows(q), :] = s * (1.0 + v * (1.0 - s))
        hgcat[inner(q), 0:C] = (v * s).astype(BF16)
        return 0
    lax.fori_loop(0, NQ, forward, 0)
    for m in range(POS // C):
        a_t[:, m * C:(m + 1) * C] = hgcat[W + m * C:W + (m + 1) * C, 0:C].T
        v_t[:, m * C:(m + 1) * C] = v_ref[m * C:(m + 1) * C, :].T

    pl.semaphore_wait(ready.at[1], 6)
    greet(ready.at[2], ahead + behind)

    loads[2].wait()
    lives = [(seq + k < n_seq).astype(F32) for k in range(3)]
    for a in range(3):
        for b in range(3):
            sw_t[a, b * C:(b + 1) * C, :] = sw_ref[a, b * C:(b + 1) * C, :].T
        tw_t[a * C:(a + 1) * C, :] = (tw_ref[a].astype(F32) * lives[a]).astype(BF16).T
    loads[3].wait()
    pl.semaphore_wait(ready.at[2], 6)
    greet(ready.at[3], ahead + behind)

    def chunk(p, n):
        for i in range(n):
            far(p + i).wait_recv()

            @pl.when(core == 0)
            def _():
                near_pass(p + i).start()
        for i in range(n):
            near_own(p + i).wait_recv()
        hg = (dot(cots[lines(p, n), :], tw_t[...]) * dsil[lines(p, n), :]).astype(BF16)
        before, after = shifted(hg.astype(F32))
        hgcat[lines(p + 1, n), 0:C] = after.astype(BF16)
        hgcat[lines(p + 1, n), C:2 * C] = hg
        hgcat[lines(p + 1, n), 2 * C:] = before.astype(BF16)

    def back(q, _):
        acc = jnp.zeros((RQ, C), F32)
        for a in range(3):
            acc = acc + dot(hgcat[pl.ds(pl.multiple_of(q * RQ + (2 - a) * W, W), RQ), :], sw_t[a])
        vg_ref[rows(q), :] = acc.astype(BF16)
        return 0

    def chunk_back(q, _):
        chunk(2 * q, 2)
        back(q - 1, 0)
        return 0

    def put(first, index, part):
        for b in range(3):
            where = pl.ds(pl.multiple_of((index * 3 + b) * C, C), C)
            value = part[:, b * C:(b + 1) * C]
            g_ref[where, :] = value if first else g_ref[where, :] + value

    def spatial(start, size, first):
        def tap(a, _):
            from_row = pl.multiple_of(start + (2 - a) * W, 32)
            put(first, a, dot(v_t[:, start:start + size], hgcat[pl.ds(from_row, size), :]))
            return 0
        return tap

    def temporal(start, size, first):
        part = dot(a_t[:, start:start + size], cots[start:start + size, :])
        put(first, 3, jnp.concatenate([part[:, k * C:(k + 1) * C] * lives[k] for k in range(3)], axis=1))

    chunk(0, 2)
    lax.fori_loop(1, 4, chunk_back, 0)
    lax.fori_loop(0, 3, spatial(0, 1024, True), 0)
    temporal(0, 1280, True)
    pl.semaphore_wait(ready.at[3], 6)
    lax.fori_loop(4, 6, chunk_back, 0)
    lax.fori_loop(0, 3, spatial(1024, 512, False), 0)
    temporal(1280, 512, False)
    chunk_back(6, 0)
    lax.fori_loop(0, 3, spatial(1536, 512, False), 0)
    temporal(1792, 256, False)
    def block(g, parity):
        return 144 * g + 72 * parity, 9 * C + 48 * g + 24 * parity

    def pair(n):
        g0, g1 = SETS[n]
        return remote(pair_out.at[g0:g1], pair_in.at[g0:g1], pair_send.at[n], pair_recv.at[n], {"seq": sibling})

    def give(n):
        for g in range(*SETS[n]):
            s_row, _ = block(g, 1 - core)
            pair_out[g, :, :] = g_ref[pl.ds(pl.multiple_of(s_row, 8), 72), :].astype(BF16)
        pair(n).start()

    pair_t = remote(pair_t_out, pair_t_in, pair_send.at[3], pair_recv.at[3], {"seq": sibling})
    chunk(14, 1)
    spatial(2048, 512, False)(2, 0)
    give(0)
    spatial(2048, 256, False)(1, 0)
    spatial(2048, 128, False)(0, 0)
    temporal(2048, 256, False)
    chunk(15, 1)
    spatial(2304, 256, False)(1, 0)
    give(1)
    temporal(2304, 256, False)
    for h in range(8):
        t_rows = [pl.ds(pl.multiple_of(block(g, 1 - core)[1], 8), 24) for g in (2 * h, 2 * h + 1)]
        pair_t_out[48 * h:48 * h + 48, :] = jnp.concatenate([g_ref[t, :] for t in t_rows], axis=0).astype(BF16)
    pair_t.start()
    spatial(2176, 256, False)(0, 0)
    give(2)

    def finish(*copies):
        for n in range(3):
            pair(n).wait_send()
        pair_t.wait_send()
        for copy in copies:
            copy.wait_send()

        def drain(p, _):
            far(p).wait_send()
            near_own(p).wait_send()
            return 0
        lax.fori_loop(0, NP, drain, 0)

    def whole(ref, sends, recvs, n):
        return remote(ref, ref, sends.at[n], recvs.at[n], {"seq": sibling})

    def take(r, n):
        high, off = heights[r], offsets[r]
        for h in range(SETS[n][0] // 2, SETS[n][1] // 2):
            s, t = [], []
            for g in (2 * h, 2 * h + 1):
                s_row, t_row = block(g, core)
                s.append(g_ref[pl.ds(pl.multiple_of(s_row + 3 * off, 8), 3 * high), :]
                         + pair_in[g, 3 * off:3 * off + 3 * high, :].astype(F32))
                t.append(g_ref[pl.ds(pl.multiple_of(t_row + off, 8), high), :]
                         + pair_t_in[24 * g + off:24 * g + off + high, :].astype(F32))
            for q in range(4):
                pieces = [i[high * q:high * q + high] for i in s] if q < 3 else t
                value = jnp.concatenate(pieces, axis=0).astype(BF16)
                for part in range(2):
                    s1_out[r][part, q, 2 * high * h:2 * high * (h + 1), :] = value[:, part * HALF:(part + 1) * HALF]

    def s1(r, part, d):
        to = ((y if part else x) + d) & 3
        return remote(s1_out[r].at[part, to], s1_in[r].at[part, d - 1], s1_send.at[r], s1_recv.at[r],
                      place(0, d, 0) if part else place(d, 0, 0))

    def of_z(r, at):
        return pl.ds(pl.multiple_of(2 * heights[r] * at, 16), 2 * heights[r])

    def s2(r, d):
        return remote(s2_out[r].at[of_z(r, (z + d) & 7)], s2_in[r].at[d - 1],
                      s2_send.at[r], s2_recv.at[r], place(0, 0, d))

    me = 4 * x + y

    def last(r, dx, dy):
        return remote(last_out[r].at[((y + dy) & 3) // 2], last_in[r].at[me], last_send.at[r], last_recv.at[r],
                      place(dx, dy, 0))

    s1_all = [whole(s1_in[r], s1_send, s1_recv, r) for r in range(n_sets)]
    s2_all = [whole(s2_in[r], s2_send, s2_recv, r) for r in range(n_sets)]
    last_all = [whole(last_in[r].at[0:15], last_send, last_recv, r) for r in range(n_sets)]
    back(6, 0)
    pair_t.wait_recv()
    for n in range(2):
        pair(n).wait_recv()
        for r in range(n_sets):
            take(r, n)
    pair(2).wait_recv()
    for r in range(n_sets):
        take(r, 2)
        for d in (2, 1, 3):
            for part in range(2):
                s1(r, part, d).start()
    back(7, 0)
    for r in range(n_sets):
        s1_all[r].wait_recv()
        for part, mine in ((0, x), (1, y)):
            total = s1_out[r][part, mine].astype(F32)
            for d in range(3):
                total = total + s1_in[r][part, d].astype(F32)
            s2_out[r][:, part * HALF:(part + 1) * HALF] = total.astype(BF16)
        for d in (4, 3, 5, 2, 6, 1, 7):
            s2(r, d).start()
    for r in range(n_sets):
        high = heights[r]
        s2_all[r].wait_recv()
        total = s2_out[r][of_z(r, z), :].astype(F32)
        for d in range(7):
            total = total + s2_in[r][d].astype(F32)
        for to in range(2):
            piece = total[high * to:high * to + high]
            last_out[r][to, :, :] = jnp.concatenate([piece[:, :HALF], piece[:, HALF:]], axis=0).astype(BF16)
        for dx, dy in PLANE:
            last(r, dx, dy).start()
        last_in[r][me, :, :] = last_out[r][y_hi]
    for r in range(n_sets):
        high, off = heights[r], offsets[r]
        last_all[r].wait_recv()
        for q in range(4):
            left = last_in[r][4 * q, 0:high, :].astype(F32)
            right = last_in[r][q, high:2 * high, :].astype(F32)
            for k in range(1, 4):
                left = left + last_in[r][4 * q + k, 0:high, :].astype(F32)
                right = right + last_in[r][4 * k + q, high:2 * high, :].astype(F32)
            out, row = (sg_ref, 3 * off + high * q) if q < 3 else (tg_ref, off)
            out[row:row + high, 0:HALF] = left * scale
            out[row:row + high, HALF:] = right * scale
    finish(*s1_all, *s2_all, *last_all)


def hand_over(*refs):
    ins, outs, sems = refs[:3], refs[3:6], refs[6]
    views = [(0, pl.ds(n * RQ, RQ)) for n in range(NQ)] + [(1, pl.ds(0, 72)), (2, pl.ds(0, 24))]
    copies = [pltpu.make_async_copy(ins[i].at[w], outs[i].at[w], sems.at[n]) for n, (i, w) in enumerate(views)]
    for copy in copies:
        copy.start()
    for copy in copies:
        copy.wait()


def compute(v, c, sw, tw, scale):
    heights = (8, 16)
    anywhere = pl.BlockSpec(memory_space=pl.ANY)
    vm = pl.BlockSpec(memory_space=pltpu.VMEM)
    dma = pltpu.SemaphoreType.DMA
    shapes = (jax.ShapeDtypeStruct((POS, C), BF16), jax.ShapeDtypeStruct((72, C), F32),
              jax.ShapeDtypeStruct((24, C), F32))
    grads = pl.pallas_call(
        functools.partial(body, scale, heights), name="block_grads",
        out_shape=tuple(pltpu.VMEM(t.shape, t.dtype) for t in shapes),
        in_specs=[anywhere] * 4, out_specs=(vm, vm, vm),
        scratch_shapes=[
            pltpu.VMEM((POS, C), BF16),
            pltpu.VMEM((3, 3 * C, C), BF16),
            pltpu.VMEM((3, C, C), BF16),
            pltpu.VMEM((POS + 2 * W, 3 * C), BF16),
            pltpu.VMEM((POS + 2 * W, 3 * C), BF16),
            pltpu.VMEM((POS, 3 * C), BF16),
            pltpu.VMEM((C, POS), BF16),
            pltpu.VMEM((C, POS), BF16),
            pltpu.VMEM((POS, C), F32),
            pltpu.VMEM((3, 3 * C, C), BF16),
            pltpu.VMEM((3 * C, C), BF16),
            pltpu.VMEM((12 * C, C), F32),
            pltpu.VMEM((16, 72, C), BF16), pltpu.VMEM((16, 72, C), BF16),
            pltpu.VMEM((384, C), BF16), pltpu.VMEM((384, C), BF16),
            *[pltpu.VMEM((2, 4, 16 * h, HALF), BF16) for h in heights],
            *[pltpu.VMEM((2, 3, 16 * h, HALF), BF16) for h in heights],
            *[pltpu.VMEM((16 * h, C), BF16) for h in heights],
            *[pltpu.VMEM((7, 2 * h, C), BF16) for h in heights],
            *[pltpu.VMEM((2, 2 * h, HALF), BF16) for h in heights],
            *[pltpu.VMEM((16, 2 * h, HALF), BF16) for h in heights],
        ] + [dma((NP,))] * 4 + [dma((4,))] * 2 + [dma((3,))] * 6 + [dma((4,)), pltpu.SemaphoreType.REGULAR((4,))],
        compiler_params=pltpu.CompilerParams(
            collective_id=0, has_side_effects=True, vmem_limit_bytes=56 * 2**20),
    )(v, c, sw, tw)
    return pl.pallas_call(
        hand_over, name="hand_over", out_shape=shapes,
        in_specs=[anywhere] * 3, out_specs=(anywhere,) * 3,
        scratch_shapes=[dma((NQ + 2,))],
    )(*[pltpu.with_memory_space_constraint(g, pltpu.VMEM) for g in grads])


def shards(video, cotangent, spatial_weight, temporal_weight):
    count = lax.axis_size("dp") * lax.axis_size("seq") * POS
    vg, sg, tg = compute(video.reshape(POS, C), cotangent.reshape(POS, C),
                         spatial_weight.reshape(3, 3 * C, C), temporal_weight, count ** -0.5)
    return vg.reshape(video.shape), sg, tg


def solution(mesh):
    placed = (P("dp", "seq", None, None, None), P("dp", "seq", None, None, None), P(), P())
    return jax.shard_map(
        shards, mesh=mesh, in_specs=placed,
        out_specs=(P("dp", "seq", None, None, None), P("seq", None), P("seq", None)),
        check_vma=False)
```

```python
import functools

import jax
import jax.numpy as jnp
from jax import lax
from jax.experimental import pallas as pl
from jax.experimental.pallas import tpu as pltpu
from jax.sharding import PartitionSpec as P

MESH = pl.DeviceIdType.MESH
H, W, C = 16, 160, 256
HALF = C // 2
POS = H * W
NQ = 8
RQ = POS // NQ
F32, BF16 = jnp.float32, jnp.bfloat16
PLANE = [(dx, dy) for dx in range(4) for dy in range(4) if dx or dy]
NP = 16
SETS = ((0, 4), (4, 10), (10, 16))


def dot(a, b):
    return lax.dot_general(a, b, (((1,), (0,)), ((), ())), preferred_element_type=F32)


def shifted(x):
    n = x.shape[0]
    col = lax.broadcasted_iota(jnp.int32, x.shape, 0) % W
    before = jnp.where(col == 0, 0.0, pltpu.roll(x, 1, 0))
    after = jnp.where(col == W - 1, 0.0, pltpu.roll(x, n - 1, 0))
    return before, after


def body(scale, stop, v_hbm, c_hbm, sw_hbm, tw_hbm, vg_ref, sg_ref, tg_ref,
         v_ref, sw_ref, tw_ref, vcat, hgcat, cots, v_t, a_t, dsil, sw_t, tw_t, g_ref,
         pair_out, pair_in, s1_out, s1_in, s2_out, s2_in, last_out, last_in,
         far_send, far_recv, near_send, near_recv, pair_send, pair_recv, s1_send, s1_recv,
         s2_send, s2_recv, last_send, last_recv, in_sems, ready):
    dp, seq = lax.axis_index("dp"), lax.axis_index("seq")
    n_seq = lax.axis_size("seq")
    core = lax.rem(seq, 2)
    x, y_lo = dp // 2, lax.rem(dp, 2)
    z, y_hi = seq // 4, lax.rem(seq // 2, 2)
    y = 2 * y_hi + y_lo
    sibling = seq + 1 - 2 * core
    prev = lax.rem(seq + n_seq - 2, n_seq)
    following = lax.rem(seq + 2, n_seq)

    def place(dx, dy, dz):
        to_x, to_y, to_z = (x + dx) & 3, (y + dy) & 3, (z + dz) & 7
        return (2 * to_x + (to_y & 1), 4 * to_z + (to_y & 2) + core)

    def rows(q):
        return pl.ds(pl.multiple_of(q * RQ, RQ), RQ)

    def inner(q):
        return pl.ds(pl.multiple_of(W + q * RQ, W), RQ)

    def lines(p, n=1):
        return pl.ds(pl.multiple_of(p * W, W), n * W)

    def remote(src, dst, send, recv, device):
        return pltpu.make_async_remote_copy(
            src_ref=src, dst_ref=dst, send_sem=send, recv_sem=recv, device_id=device, device_id_type=MESH)

    def far(p):
        return remote(c_hbm.at[lines(p)], cots.at[lines(p), pl.ds(2 * C, C)],
                      far_send.at[p], far_recv.at[p], {"seq": prev})

    def near_own(p):
        return remote(c_hbm.at[lines(p)], cots.at[lines(p), pl.ds(C, C)],
                      near_send.at[p], near_recv.at[p], {"seq": sibling})

    def near_pass(p):
        return remote(cots.at[lines(p), pl.ds(2 * C, C)], cots.at[lines(p), pl.ds(C, C)],
                      near_send.at[p], near_recv.at[p], {"seq": sibling})

    ahead = (place(1, 0, 0), place(0, 1, 0), place(0, 0, 1))
    behind = (place(3, 0, 0), place(0, 3, 0), place(0, 0, 7))

    def greet(sem, devices):
        for device in devices:
            pl.semaphore_signal(sem, inc=1, device_id=device, device_id_type=MESH)

    barrier = pltpu.get_barrier_semaphore()
    greet(barrier, ({"seq": following}, {"seq": sibling}) + ahead)
    loads = [pltpu.make_async_copy(v_hbm, v_ref, in_sems.at[0]),
             pltpu.make_async_copy(sw_hbm, sw_ref, in_sems.at[1]),
             pltpu.make_async_copy(tw_hbm, tw_ref, in_sems.at[2]),
             pltpu.make_async_copy(c_hbm, cots.at[:, pl.ds(0, C)], in_sems.at[3])]
    for load in loads:
        load.start()
    pl.semaphore_wait(barrier, 5)
    if stop == "b":
        for load in loads:
            load.wait()
        return
    for p in range(NP):
        far(p).start()

    @pl.when(core == 1)
    def _():
        for p in range(NP):
            near_own(p).start()
    greet(ready.at[0], behind)

    zero = jnp.zeros((W, 3 * C), BF16)
    for ref in (vcat, hgcat):
        ref[0:W, :] = zero
        ref[W + POS:2 * W + POS, :] = zero
    loads[0].wait()

    def spread(q, _):
        v = v_ref[rows(q), :]
        before, after = shifted(v.astype(F32))
        vcat[inner(q), 0:C] = before.astype(BF16)
        vcat[inner(q), C:2 * C] = v
        vcat[inner(q), 2 * C:] = after.astype(BF16)
        return 0
    lax.fori_loop(0, NQ, spread, 0)
    loads[1].wait()
    pl.semaphore_wait(ready.at[0], 3)
    greet(ready.at[1], ahead + behind)

    def forward(q, _):
        acc = jnp.zeros((RQ, C), F32)
        for a in range(3):
            acc = acc + dot(vcat[pl.ds(pl.multiple_of(q * RQ + a * W, W), RQ), :], sw_ref[a])
        v = acc.astype(BF16).astype(F32)
        s = 1.0 / (1.0 + jnp.exp(-v))
        dsil[rows(q), :] = s * (1.0 + v * (1.0 - s))
        hgcat[inner(q), 0:C] = (v * s).astype(BF16)
        return 0
    lax.fori_loop(0, NQ, forward, 0)
    for m in range(POS // C):
        a_t[:, m * C:(m + 1) * C] = hgcat[W + m * C:W + (m + 1) * C, 0:C].T
        v_t[:, m * C:(m + 1) * C] = v_ref[m * C:(m + 1) * C, :].T

    pl.semaphore_wait(ready.at[1], 6)
    greet(ready.at[2], ahead + behind)

    loads[2].wait()
    lives = [(seq + k < n_seq).astype(F32) for k in range(3)]
    for a in range(3):
        for b in range(3):
            sw_t[a, b * C:(b + 1) * C, :] = sw_ref[a, b * C:(b + 1) * C, :].T
        tw_t[a * C:(a + 1) * C, :] = (tw_ref[a].astype(F32) * lives[a]).astype(BF16).T
    loads[3].wait()
    pl.semaphore_wait(ready.at[2], 6)
    greet(ready.at[3], ahead + behind)

    def chunk(p, n):
        for i in range(n):
            far(p + i).wait_recv()

            @pl.when(core == 0)
            def _():
                near_pass(p + i).start()
        for i in range(n):
            near_own(p + i).wait_recv()
        hg = (dot(cots[lines(p, n), :], tw_t[...]) * dsil[lines(p, n), :]).astype(BF16)
        before, after = shifted(hg.astype(F32))
        hgcat[lines(p + 1, n), 0:C] = after.astype(BF16)
        hgcat[lines(p + 1, n), C:2 * C] = hg
        hgcat[lines(p + 1, n), 2 * C:] = before.astype(BF16)

    def back(q, _):
        acc = jnp.zeros((RQ, C), F32)
        for a in range(3):
            acc = acc + dot(hgcat[pl.ds(pl.multiple_of(q * RQ + (2 - a) * W, W), RQ), :], sw_t[a])
        vg_ref[rows(q), :] = acc.astype(BF16)
        return 0

    def chunk_back(q, _):
        chunk(2 * q, 2)
        back(q - 1, 0)
        return 0

    def put(first, index, part):
        for b in range(3):
            where = pl.ds(pl.multiple_of((index * 3 + b) * C, C), C)
            value = part[:, b * C:(b + 1) * C]
            g_ref[where, :] = value if first else g_ref[where, :] + value

    def spatial(start, size, first):
        def tap(a, _):
            from_row = pl.multiple_of(start + (2 - a) * W, 32)
            put(first, a, dot(v_t[:, start:start + size], hgcat[pl.ds(from_row, size), :]))
            return 0
        return tap

    def temporal(start, size, first):
        part = dot(a_t[:, start:start + size], cots[start:start + size, :])
        put(first, 3, jnp.concatenate([part[:, k * C:(k + 1) * C] * lives[k] for k in range(3)], axis=1))

    chunk(0, 2)
    lax.fori_loop(1, 4, chunk_back, 0)
    lax.fori_loop(0, 3, spatial(0, 1024, True), 0)
    temporal(0, 1280, True)
    pl.semaphore_wait(ready.at[3], 6)
    lax.fori_loop(4, 6, chunk_back, 0)
    lax.fori_loop(0, 3, spatial(1024, 512, False), 0)
    temporal(1280, 512, False)
    chunk_back(6, 0)
    lax.fori_loop(0, 3, spatial(1536, 512, False), 0)
    temporal(1792, 256, False)
    chunk(14, 1)
    temporal(2048, 256, False)
    chunk(15, 1)
    temporal(2304, 256, False)

    def block(g, parity):
        return 144 * g + 72 * parity, 9 * C + 48 * g + 24 * parity

    def give(g):
        s_row, t_row = block(g, 1 - core)
        pair_out[g, 0:72, :] = g_ref[pl.ds(pl.multiple_of(s_row, 8), 72), :].astype(BF16)
        pair_out[g, 72:96, :] = g_ref[pl.ds(pl.multiple_of(t_row, 8), 24), :].astype(BF16)

    def pair(n):
        g0, g1 = SETS[n]
        return remote(pair_out.at[g0:g1], pair_in.at[g0:g1], pair_send.at[n], pair_recv.at[n], {"seq": sibling})

    final_tap = spatial(2048, 512, False)
    for n in range(3):
        final_tap(n, 0)
        for g in range(*SETS[n]):
            give(g)
        pair(n).start()
    back(6, 0)

    def finish(*copies):
        for n in range(3):
            pair(n).wait_send()
        for copy in copies:
            copy.wait_send()

        def drain(p, _):
            far(p).wait_send()
            near_own(p).wait_send()
            return 0
        lax.fori_loop(0, NP, drain, 0)

    def whole(ref, sends, recvs, n):
        return remote(ref, ref, sends.at[n], recvs.at[n], {"seq": sibling})

    def take(r, n):
        for h in range(SETS[n][0] // 2, SETS[n][1] // 2):
            s, t = [], []
            for g in (2 * h, 2 * h + 1):
                s_row, t_row = block(g, core)
                s.append(g_ref[pl.ds(pl.multiple_of(s_row + 24 * r, 8), 24), :]
                         + pair_in[g, 24 * r:24 * r + 24, :].astype(F32))
                t.append(g_ref[pl.ds(pl.multiple_of(t_row + 8 * r, 8), 8), :]
                         + pair_in[g, 72 + 8 * r:80 + 8 * r, :].astype(F32))
            for q in range(4):
                value = jnp.concatenate([i[8 * q:8 * q + 8] for i in s] if q < 3 else t, axis=0).astype(BF16)
                for part in range(2):
                    s1_out[r, part, q, 16 * h:16 * h + 16, :] = value[:, part * HALF:(part + 1) * HALF]

    def s1(r, part, d):
        to = ((y if part else x) + d) & 3
        return remote(s1_out.at[r, part, to], s1_in.at[r, part, d - 1], s1_send.at[r], s1_recv.at[r],
                      place(0, d, 0) if part else place(d, 0, 0))

    def s2(r, d):
        return remote(s2_out.at[r, pl.ds(pl.multiple_of(16 * ((z + d) & 7), 16), 16)], s2_in.at[r, d - 1],
                      s2_send.at[r], s2_recv.at[r], place(0, 0, d))

    me = 4 * x + y

    def last(r, dx, dy):
        return remote(last_out.at[r, ((y + dy) & 3) // 2], last_in.at[r, me], last_send.at[r], last_recv.at[r],
                      place(dx, dy, 0))

    s1_all = [whole(s1_in.at[r], s1_send, s1_recv, r) for r in range(3)]
    s2_all = [whole(s2_in.at[r], s2_send, s2_recv, r) for r in range(3)]
    last_all = [whole(last_in.at[r, 0:15], last_send, last_recv, r) for r in range(3)]
    for n in range(2):
        pair(n).wait_recv()
        for r in range(3):
            take(r, n)
    pair(2).wait_recv()
    if stop == "p":
        back(7, 0)
        finish()
        return
    for r in range(3):
        take(r, 2)
        for d in (2, 1, 3):
            for part in range(2):
                s1(r, part, d).start()
    back(7, 0)
    for r in range(3):
        s1_all[r].wait_recv()
        for part, mine in ((0, x), (1, y)):
            total = s1_out[r, part, mine].astype(F32)
            for d in range(3):
                total = total + s1_in[r, part, d].astype(F32)
            s2_out[r, :, part * HALF:(part + 1) * HALF] = total.astype(BF16)
        for d in (4, 3, 5, 2, 6, 1, 7):
            s2(r, d).start()
    for r in range(3):
        s2_all[r].wait_recv()
        total = s2_out[r, pl.ds(pl.multiple_of(16 * z, 16), 16), :].astype(F32)
        for d in range(7):
            total = total + s2_in[r, d].astype(F32)
        for to in range(2):
            piece = total[8 * to:8 * to + 8]
            last_out[r, to, :, :] = jnp.concatenate([piece[:, :HALF], piece[:, HALF:]], axis=0).astype(BF16)
        for dx, dy in PLANE:
            last(r, dx, dy).start()
        last_in[r, me, :, :] = last_out[r, y_hi]
    for r in range(3):
        last_all[r].wait_recv()
        for q in range(4):
            left = last_in[r, 4 * q, 0:8, :].astype(F32)
            right = last_in[r, q, 8:16, :].astype(F32)
            for k in range(1, 4):
                left = left + last_in[r, 4 * q + k, 0:8, :].astype(F32)
                right = right + last_in[r, 4 * k + q, 8:16, :].astype(F32)
            out, row = (sg_ref, 24 * r + 8 * q) if q < 3 else (tg_ref, 8 * r)
            out[row:row + 8, 0:HALF] = left * scale
            out[row:row + 8, HALF:] = right * scale
    finish(*s1_all, *s2_all, *last_all)


def hand_over(*refs):
    ins, outs, sems = refs[:3], refs[3:6], refs[6]
    views = [(0, pl.ds(n * RQ, RQ)) for n in range(NQ)] + [(1, pl.ds(0, 72)), (2, pl.ds(0, 24))]
    copies = [pltpu.make_async_copy(ins[i].at[w], outs[i].at[w], sems.at[n]) for n, (i, w) in enumerate(views)]
    for copy in copies:
        copy.start()
    for copy in copies:
        copy.wait()


def compute(v, c, sw, tw, scale, stop=None, cid=0):
    anywhere = pl.BlockSpec(memory_space=pl.ANY)
    vm = pl.BlockSpec(memory_space=pltpu.VMEM)
    dma = pltpu.SemaphoreType.DMA
    shapes = (jax.ShapeDtypeStruct((POS, C), BF16), jax.ShapeDtypeStruct((72, C), F32),
              jax.ShapeDtypeStruct((24, C), F32))
    grads = pl.pallas_call(
        functools.partial(body, scale, stop), name=f"block_grads{'' if stop is None else stop}",
        out_shape=tuple(pltpu.VMEM(t.shape, t.dtype) for t in shapes),
        in_specs=[anywhere] * 4, out_specs=(vm, vm, vm),
        scratch_shapes=[
            pltpu.VMEM((POS, C), BF16),
            pltpu.VMEM((3, 3 * C, C), BF16),
            pltpu.VMEM((3, C, C), BF16),
            pltpu.VMEM((POS + 2 * W, 3 * C), BF16),
            pltpu.VMEM((POS + 2 * W, 3 * C), BF16),
            pltpu.VMEM((POS, 3 * C), BF16),
            pltpu.VMEM((C, POS), BF16),
            pltpu.VMEM((C, POS), BF16),
            pltpu.VMEM((POS, C), F32),
            pltpu.VMEM((3, 3 * C, C), BF16),
            pltpu.VMEM((3 * C, C), BF16),
            pltpu.VMEM((12 * C, C), F32),
            pltpu.VMEM((16, 96, C), BF16), pltpu.VMEM((16, 96, C), BF16),
            pltpu.VMEM((3, 2, 4, 128, HALF), BF16), pltpu.VMEM((3, 2, 3, 128, HALF), BF16),
            pltpu.VMEM((3, 128, C), BF16), pltpu.VMEM((3, 7, 16, C), BF16),
            pltpu.VMEM((3, 2, 16, HALF), BF16), pltpu.VMEM((3, 16, 16, HALF), BF16),
        ] + [dma((NP,))] * 4 + [dma((3,))] * 8 + [dma((4,)), pltpu.SemaphoreType.REGULAR((4,))],
        compiler_params=pltpu.CompilerParams(
            collective_id=cid, has_side_effects=True, vmem_limit_bytes=56 * 2**20),
    )(v, c, sw, tw)
    return pl.pallas_call(
        hand_over, name="hand_over", out_shape=shapes,
        in_specs=[anywhere] * 3, out_specs=(anywhere,) * 3,
        scratch_shapes=[dma((NQ + 2,))],
    )(*[pltpu.with_memory_space_constraint(g, pltpu.VMEM) for g in grads])


def shards(video, cotangent, spatial_weight, temporal_weight):
    count = lax.axis_size("dp") * lax.axis_size("seq") * POS
    vg, sg, tg = compute(video.reshape(POS, C), cotangent.reshape(POS, C),
                         spatial_weight.reshape(3, 3 * C, C), temporal_weight, count ** -0.5)
    return vg.reshape(video.shape), sg, tg


def solution(mesh):
    placed = (P("dp", "seq", None, None, None), P("dp", "seq", None, None, None), P(), P())
    return jax.shard_map(
        shards, mesh=mesh, in_specs=placed,
        out_specs=(P("dp", "seq", None, None, None), P("seq", None), P("seq", None)),
        check_vma=False)
```
